32 devices in a mesh: dp: 4 (over y, x), item: 8 (over z, core).
Axes of the slice: x: 2, y: 2, z: 4, core: 2. Of those that a mesh axis runs over, the one named last changes fastest.
Arguments:
- queries: bfloat16 [32768, 256], P(('dp', 'item')), may hold values from -0.5 to 0.5
- item_table: float32 [32768, 256], P('item'), may hold values from -0.5 to 0.5
- adagrad_state: float32 [32768], P('item'), may hold values from 1 to 1000
- pos_owner: int32 [32768, 1], P(('dp', 'item')), may hold values from 0 to 7; in each aligned block of 1024 rows (0 to 1023, 1024 to 2047, ...) at most 384 rows name the same one
- pos_row: int32 [32768], P(('dp', 'item')), may hold values from 0 to 4095
- neg_rows: int32 [1536], P(('dp', 'item')), may hold values from 0 to 4095
Outputs:
- query_grad: bfloat16 [32768, 256], P(('dp', 'item'))
- example_loss: float32 [32768], P(('dp', 'item'))
- new_table: float32 [32768, 256], P('item')
- new_state: float32 [32768], P('item')
The draws below stay inside these ranges and needn't reach their ends.
Inputs may be any that keep to these rules, and one draw needn't show every extreme that they name: `pos_owner`: within the rows of one device (aligned blocks of 1024 examples) no shard is named more than 384 times; some device's block names one shard exactly 384 times.
All inputs are finite; a program needn't handle non-finite values.
Results may differ from the reference program's by a relative error of at most 0.0049.
Values may be sent and summed in bfloat16 or wider, within the bound.
No kernel may reach another device: no remote copies, remote signals or barrier semaphores. Data moves between devices by JAX's collectives and lax.ppermute only.
A program may use at most 64 MiB of HBM per device.

```python
import math
import jax
import jax.numpy as jnp
import numpy as np
from jax import lax

D = 256
ROWS_DEV = 4096
EX_DEV = 1024
NEG_DEV = 48
CAP = 384
TABLE_ROWS = 32768
EXAMPLES = 32768
NEGS = 1536
N_ITEM = 8


def with_ends(values, stream_key, smallest, largest):
    dims = values.shape
    place = [jax.random.randint(jax.random.fold_in(stream_key, axis), (), 0, dims[axis]) for axis in range(len(dims))]
    values = values.at[tuple(place)].set(smallest)
    longest = dims.index(max(dims))
    place[longest] = (place[longest] + 1) % dims[longest]
    return values.at[tuple(place)].set(largest)


def shard_levels(key, dims, cuts, least, high):
    gain, own = 1.0, jax.random.fold_in(key, 6)
    for position, parts in cuts:
        steps = jnp.exp(jax.random.uniform(jax.random.fold_in(own, position), (parts,), jnp.float32, least / len(cuts), high / len(cuts)))
        gain = gain * jnp.repeat(steps, dims[position] // parts).reshape([-1 if axis == position else 1 for axis in range(len(dims))])
    return gain


def routed_block(rng, own, number, rows, number_of, top, most, skew):
    ranking = jax.random.permutation(rng, number_of)
    crowded, usual = portions_of(number_of, rows * top, most, skew, True), portions_of(number_of, rows * top, most, skew, False)
    places = jnp.arange(number_of)

    def named(sizes, turn):
        used = int((sizes > 0).sum())
        fixed = max(1, used // 4)
        shifted = fixed + (places - fixed + turn * (used - fixed)) % max(1, number_of - fixed)
        return jnp.zeros((number_of,), jnp.int32).at[ranking[jnp.where(places < fixed, places, shifted)]].set(jnp.asarray(sizes, jnp.int32))

    sizes = jnp.where(number % 4 == 0, named(crowded, number // 4), named(usual, number - number // 4 - 1))
    mixed = jax.random.permutation(jax.random.fold_in(own, 3), number_of)
    giver, sink = mixed[0:number_of // 2 * 2:2], mixed[1:number_of // 2 * 2:2]
    slack = jnp.minimum(sizes[giver] - 1, most - sizes[sink]) // 2
    slack = jnp.where((giver == ranking[0]) | (sink == ranking[0]) | (sizes[sink] == 0), 0, jnp.maximum(slack, 0))
    shifted = jax.random.randint(jax.random.fold_in(own, 4), (number_of // 2,), 0, 1 << 20) % (slack + 1)
    sizes = sizes.at[giver].add(-shifted).at[sink].add(shifted)
    items = jnp.searchsorted(jnp.cumsum(sizes), jnp.arange(rows * top), side="right").astype(jnp.int32)
    listing = items.reshape(top, rows).T
    listing = listing[jax.random.permutation(jax.random.fold_in(own, 1), rows)]
    turn = jax.random.randint(jax.random.fold_in(own, 2), (rows, 1), 0, top)
    return jnp.take_along_axis(listing, (jnp.arange(top)[None, :] + turn) % top, axis=1)


def portions_of(amount, total, limit, lean, full):
    weights = [(1 << 20) // math.isqrt(grade ** lean) + 1 for grade in range(1, amount + 1)]
    largest = limit if full else min(limit, max(-(-total // amount), total * weights[0] // sum(weights)))
    least = 1 if total - largest >= amount - 1 else 0
    holding, surplus = [largest] + [least] * (amount - 1), total - largest - least * (amount - 1)
    while surplus > 0:
        candidates = [i for i in range(1, amount) if holding[i] < largest] or [i for i in range(1, amount) if holding[i] < limit]
        mass, left = sum([weights[i] for i in candidates]), surplus
        for i in candidates:
            addition = min(limit - holding[i], max(1, left * weights[i] // mass), surplus)
            holding[i] = holding[i] + addition
            surplus = surplus - addition
    return np.array(holding)


def gaussian(rng, extent, deviation, most, cuts=(), kind=jnp.bfloat16):
    gain = shard_levels(rng, extent, cuts, -0.22, 0.18) if cuts else 1.0
    result = jax.random.normal(rng, extent, jnp.float32) * deviation * gain
    return jnp.minimum(jnp.maximum(result, -most), most).astype(kind)


def setup_inputs(seed: int = 0) -> dict:
    seeds = jax.random.split(jax.random.key(seed), 7)
    queries = gaussian(seeds[0], (EXAMPLES, D), 0.0625, 0.5, ((0, 32),))
    item_table = gaussian(seeds[1], (TABLE_ROWS, D), 0.0625, 0.5, ((0, 8),), jnp.float32)
    adagrad_state = jnp.clip(jnp.exp(math.log(1000.0) - 6.9077553 * jax.random.uniform(seeds[2], (TABLE_ROWS,), jnp.float32) ** shard_levels(seeds[2], (TABLE_ROWS,), ((0, 8),), -0.2, 0.2)), 1.0, 1000.0)
    pos_owner_keys = jax.random.split(jax.random.fold_in(seeds[3], 1), EXAMPLES // EX_DEV)
    pos_owner_turns = jax.random.permutation(jax.random.fold_in(seeds[3], 3), EXAMPLES // EX_DEV)
    pos_owner = jax.vmap(lambda own, number: routed_block(jax.random.fold_in(seeds[3], 2), own, number, EX_DEV, N_ITEM, 1, CAP, 2))(pos_owner_keys, pos_owner_turns).reshape((EXAMPLES, 1))
    pos_row = with_ends(jax.random.randint(seeds[4], (EXAMPLES,), 0, ROWS_DEV), jax.random.fold_in(seeds[4], 1), 0, ROWS_DEV - 1).astype(jnp.int32)
    neg_rows = with_ends(jax.random.randint(seeds[5], (NEGS,), 0, ROWS_DEV), jax.random.fold_in(seeds[5], 1), 0, ROWS_DEV - 1).astype(jnp.int32)
    return dict(queries=queries, item_table=item_table, adagrad_state=adagrad_state, pos_owner=pos_owner, pos_row=pos_row, neg_rows=neg_rows)


INV_TEMP = 20.0
LEARN_RATE = 0.05
EPSILON = 1e-06

def unit_rows(matrix):
    row_norm = jnp.sqrt(lax.optimization_barrier(jnp.sum(matrix * matrix, axis=-1, keepdims=True)) + EPSILON)
    return (matrix / row_norm, row_norm)

def reference(queries, item_table, adagrad_state, pos_owner, pos_row, neg_rows):
    query_f = queries.astype(jnp.float32)
    query_hat, query_norm = unit_rows(query_f)
    unit_table, table_norm = unit_rows(item_table)
    table_send = unit_table.astype(jnp.bfloat16)
    query_send = query_hat.astype(jnp.bfloat16)
    pos_gid = (pos_owner[:, 0] * ROWS_DEV + pos_row).astype(jnp.int32)
    neg_owner = jnp.arange(NEGS, dtype=jnp.int32) // NEG_DEV % N_ITEM
    neg_gid = (neg_owner * ROWS_DEV + neg_rows).astype(jnp.int32)
    neg_e = table_send[neg_gid]
    pos_e = table_send[pos_gid]
    blocks = EXAMPLES // EX_DEV

    def one_block(carry, pieces):
        q_send, q_hat, q_norm, p_e, p_gid = pieces
        scores = jnp.dot(q_send, neg_e.T, preferred_element_type=jnp.float32) * INV_TEMP
        allowed = neg_gid[None, :] != p_gid[:, None]
        s_pos = INV_TEMP * lax.optimization_barrier(jnp.sum(q_send.astype(jnp.float32) * p_e.astype(jnp.float32), axis=1))
        totals = jnp.exp(s_pos) + lax.optimization_barrier(jnp.sum(jnp.where(allowed, jnp.exp(scores), 0.0), axis=1))
        lse = jnp.log(totals)
        loss = lse - s_pos
        probs = jnp.where(allowed, jnp.exp(scores - lse[:, None]), 0.0).astype(jnp.bfloat16)
        p_pos = jnp.exp(s_pos - lse)
        g_q = INV_TEMP * ((p_pos - 1.0)[:, None] * p_e.astype(jnp.float32) + jnp.dot(probs, neg_e, preferred_element_type=jnp.float32))
        q_grad = ((g_q - q_hat * lax.optimization_barrier(jnp.sum(q_hat * g_q, axis=1, keepdims=True))) / q_norm).astype(jnp.bfloat16)
        g_pos = INV_TEMP * (p_pos - 1.0)[:, None] * q_hat
        carry = carry + INV_TEMP * jnp.dot(probs.T, q_send, preferred_element_type=jnp.float32)
        return (carry, (q_grad, loss, g_pos))
    pieces = (query_send.reshape(blocks, EX_DEV, D), query_hat.reshape(blocks, EX_DEV, D), query_norm.reshape(blocks, EX_DEV, 1), pos_e.reshape(blocks, EX_DEV, D), pos_gid.reshape(blocks, EX_DEV))
    g_neg, (q_grad, loss, g_pos) = lax.scan(one_block, jnp.zeros((NEGS, D), jnp.float32), pieces)
    g_unit = jnp.zeros((TABLE_ROWS, D), jnp.float32)
    g_unit = g_unit.at[pos_gid].add(g_pos.reshape(EXAMPLES, D))
    g_unit = g_unit.at[neg_gid].add(g_neg)
    g_row = (g_unit - unit_table * lax.optimization_barrier(jnp.sum(unit_table * g_unit, axis=1, keepdims=True))) / table_norm
    new_state = adagrad_state + lax.optimization_barrier(jnp.mean(g_row * g_row, axis=1))
    new_table = item_table - LEARN_RATE * g_row / jnp.sqrt(new_state)[:, None]
    return (q_grad.reshape(EXAMPLES, D), loss.reshape(EXAMPLES), new_table, new_state)
```

```python
import math

import jax
import jax.numpy as jnp
from jax import lax
from jax.experimental import pallas as pl
from jax.experimental.pallas import tpu as pltpu
from jax.sharding import PartitionSpec as P

INV_TEMP = 20.0
LEARN_RATE = 0.05
EPSILON = 1e-06
F32 = jnp.float32
BF16 = jnp.bfloat16
NT = (((1,), (1,)), ((), ()))


def unit_rows(matrix):
    row_norm = jnp.sqrt(jnp.sum(matrix * matrix, axis=-1, keepdims=True) + EPSILON)
    return (matrix / row_norm, row_norm)


def iota(shape, axis):
    return lax.broadcasted_iota(jnp.int32, shape, axis).astype(F32)


def to_sub(row):
    return jnp.transpose(jnp.broadcast_to(row, (128, row.shape[1])))[:, :1]


def to_lane(col):
    return jnp.transpose(jnp.broadcast_to(col, (col.shape[0], 128)))[:1, :]


def one_hot(test):
    return jnp.where(test, 1.0, 0.0).astype(BF16)


def earlier_count(mask):
    total, step = mask, 1
    lane = lax.broadcasted_iota(jnp.int32, mask.shape, 1)
    while step < mask.shape[1]:
        total = total + jnp.where(lane >= step, pltpu.roll(total, step, axis=1), 0.0)
        step *= 2
    return total - mask


def rows_at(start, size):
    return pl.ds(pl.multiple_of(start * size, size), size)


def route_kernel(me_ref, gid_ref, own_ref, table_ref, found_ref, rank_ref, rid_ref, place_ref, send_ref):
    blocks, examples = gid_ref.shape
    table_rows = table_ref.shape[0]
    slots = rid_ref.shape[1]
    chunk = math.gcd(table_rows, 512)
    base = me_ref[0] * table_rows

    def normalize(step, carry):
        part = table_ref[rows_at(step, chunk), :]
        send_ref[rows_at(step, chunk), :] = unit_rows(part)[0].astype(BF16)
        return carry

    lax.fori_loop(0, table_rows // chunk, normalize, 0)
    local = gid_ref[...] - base
    mine = jnp.logical_and(local >= 0, local < table_rows)
    rank = earlier_count(jnp.where(mine, 1.0, 0.0))
    rank_ref[...] = jnp.where(mine, rank, -1.0)
    local = local.astype(F32)

    owner = lax.broadcasted_iota(jnp.int32, (blocks, examples), 0)
    own = own_ref[...]
    named = jnp.logical_and(own >= owner * table_rows, own < (owner + 1) * table_rows)
    count = earlier_count(jnp.where(named, 1.0, 0.0))
    spot = jnp.where(named, count + owner.astype(F32) * slots, 0.0)
    place_ref[...] = jnp.sum(spot, axis=0, keepdims=True)

    for block in range(blocks):
        chosen = iota((slots, examples), 0) == rank_ref[block : block + 1, :]
        wanted = jnp.sum(
            jnp.where(chosen, local[block : block + 1, :], 0.0), axis=1, keepdims=True
        )
        rid_ref[block : block + 1, :] = to_lane(wanted)

    def find(block, carry):
        wanted = to_sub(rid_ref[pl.ds(block, 1), :])

        def gather(step, total):
            pick = one_hot(wanted - (step * chunk).astype(F32) == iota((slots, chunk), 1))
            return total + jnp.dot(
                pick, send_ref[rows_at(step, chunk), :], preferred_element_type=F32
            )

        total = lax.fori_loop(
            0, table_rows // chunk, gather, jnp.zeros((slots, table_ref.shape[1]), F32)
        )
        found_ref[rows_at(block, slots), :] = total.astype(BF16)
        return carry

    lax.fori_loop(0, blocks, find, 0)


def owner_kernel(count, first, me_ref, *refs):
    queries, refs = refs[:count], refs[count:]
    rank_ref, rid_ref, found_ref, negs_ref, nid_ref, refs = *refs[:5], refs[5:]
    prior_ref = None
    if not first:
        prior_ref, refs = refs[0], refs[1:]
    pull_ref, outrid_ref, neg_ref, held, nsub, exps, copy_sem = refs
    slots = rid_ref.shape[1]
    examples = held.shape[1]
    negs = negs_ref.shape[0]
    chunk = math.gcd(negs, 256)
    copies = [
        pltpu.make_async_copy(query, held.at[spot], copy_sem.at[spot])
        for spot, query in enumerate(queries)
    ]
    for copy in copies:
        copy.start()
    for step in range(negs // chunk):
        part = nid_ref[:, step * chunk : (step + 1) * chunk]
        nsub[step * chunk : (step + 1) * chunk, :] = jnp.broadcast_to(to_sub(part), (chunk, 128))
    if first:
        neg_ref[...] = jnp.zeros_like(neg_ref)
    else:
        neg_ref[...] = prior_ref[...]
    for copy in copies:
        copy.wait()

    def block_step(spot, carry):
        source = me_ref[1 + spot]
        rank = rank_ref[pl.ds(source, 1), :]
        rid = rid_ref[pl.ds(source, 1), :]
        outrid_ref[pl.ds(spot, 1), :] = rid
        pick = one_hot(iota((slots, examples), 0) == rank)
        query_hat, _ = unit_rows(jnp.dot(pick, held[spot], preferred_element_type=F32))
        query_send = query_hat.astype(BF16)
        pos_e = found_ref[rows_at(source, slots), :].astype(F32)
        s_pos = INV_TEMP * jnp.sum(query_send.astype(F32) * pos_e, axis=1, keepdims=True)
        pos_exp = to_lane(jnp.exp(s_pos))

        def add_exp(step, total):
            scores = INV_TEMP * lax.dot_general(
                negs_ref[rows_at(step, chunk), :], query_send, NT, preferred_element_type=F32
            )
            keep = nsub[rows_at(step, chunk), :][:, :1] != rid
            part = jnp.where(keep, jnp.exp(scores), 0.0)
            exps[rows_at(step, chunk), :] = part
            return total + jnp.sum(part, axis=0, keepdims=True)

        total = lax.fori_loop(0, negs // chunk, add_exp, pos_exp)
        scale = 1.0 / total

        def add_grad(step, inner):
            probs = (exps[rows_at(step, chunk), :] * scale).astype(BF16)
            neg_ref[rows_at(step, chunk), :] += jnp.dot(
                probs, query_send, preferred_element_type=F32
            )
            return inner

        lax.fori_loop(0, negs // chunk, add_grad, 0)
        p_pos = to_sub(pos_exp * scale)
        pull_ref[rows_at(spot, slots), :] = (INV_TEMP * (p_pos - 1.0) * query_hat).astype(BF16)
        return carry

    lax.fori_loop(0, count, block_step, 0)


def scatter_kernel(pieces, *refs):
    pulls, rids, dense_ref = refs[:pieces], refs[pieces : 2 * pieces], refs[2 * pieces]
    rows = dense_ref.shape[0]
    offset = (pl.program_id(0) * rows).astype(F32)
    total = jnp.zeros(dense_ref.shape, F32)
    for pull_ref, rid_ref in zip(pulls, rids):
        count, slots = rid_ref.shape
        ids = jnp.concatenate([rid_ref[spot : spot + 1, :] for spot in range(count)], axis=1)
        put = one_hot(iota((rows, count * slots), 0) == ids - offset)
        total = total + jnp.dot(put, pull_ref[...], preferred_element_type=F32)
    dense_ref[...] = total.astype(BF16)


def home_kernel(query_ref, place_ref, gid_ref, back_ref, negs_ref, nid_ref, grad_ref, loss_ref):
    examples = query_ref.shape[0]
    spots = back_ref.shape[0]
    pick = one_hot(iota((examples, spots), 1) == to_sub(place_ref[...]))
    pos_e = jnp.dot(pick, back_ref[...], preferred_element_type=F32)
    query_hat, query_norm = unit_rows(query_ref[...].astype(F32))
    query_send = query_hat.astype(BF16)
    s_pos = INV_TEMP * jnp.sum(query_send.astype(F32) * pos_e, axis=1, keepdims=True)
    pos_exp = jnp.exp(s_pos)
    scores = INV_TEMP * lax.dot_general(
        query_send, negs_ref[...], NT, preferred_element_type=F32
    )
    keep = nid_ref[...] != to_sub(gid_ref[...])
    part = jnp.where(keep, jnp.exp(scores), 0.0)
    total = pos_exp + jnp.sum(part, axis=1, keepdims=True)
    scale = 1.0 / total
    loss_ref[...] = to_lane(jnp.log(total) - s_pos)
    probs = (part * scale).astype(BF16)
    g_query = INV_TEMP * (
        (pos_exp * scale - 1.0) * pos_e
        + jnp.dot(probs, negs_ref[...], preferred_element_type=F32)
    )
    along = jnp.sum(query_hat * g_query, axis=1, keepdims=True)
    grad_ref[...] = ((g_query - query_hat * along) / query_norm).astype(BF16)


def update_kernel(table_ref, state_ref, pull_ref, neg_ref, row_ref, new_ref, new_state_ref):
    rows = table_ref.shape[0]
    offset = (pl.program_id(0) * rows).astype(F32)
    put = one_hot(iota((rows, row_ref.shape[1]), 0) == row_ref[...] - offset)
    g_unit = pull_ref[...].astype(F32) + jnp.dot(put, neg_ref[...], preferred_element_type=F32)
    table = table_ref[...]
    unit, norm = unit_rows(table)
    g_row = (g_unit - unit * jnp.sum(unit * g_unit, axis=1, keepdims=True)) / norm
    state = to_sub(state_ref[...]) + jnp.mean(g_row * g_row, axis=1, keepdims=True)
    new_state_ref[...] = to_lane(state)
    new_ref[...] = table - LEARN_RATE * g_row / jnp.sqrt(state)


def whole(ndim=2):
    return pl.BlockSpec(memory_space=pltpu.VMEM)


def flip(name, count, bit):
    return [(index, index ^ (1 << bit)) for index in range(count)]


def halve(value, name, count, bit):
    half = value.shape[0] // 2
    mine = (lax.axis_index(name) >> bit) & 1
    give = lax.dynamic_slice_in_dim(value, (1 - mine) * half, half, 0)
    keep = lax.dynamic_slice_in_dim(value, mine * half, half, 0)
    got = lax.ppermute(give, name, flip(name, count, bit))
    return (keep.astype(F32) + got.astype(F32)).astype(BF16)


def double(value, name, count, bit):
    mine = (lax.axis_index(name) >> bit) & 1
    got = lax.ppermute(value, name, flip(name, count, bit))
    low = jnp.concatenate([value, got], axis=0)
    high = jnp.concatenate([got, value], axis=0)
    return jnp.where(mine == 0, low, high)


def to_all(value, name, count):
    copies = jnp.broadcast_to(value[None], (count, *value.shape))
    return lax.all_to_all(copies, name, split_axis=0, concat_axis=0, tiled=True)


def on_device(queries, item_table, adagrad_state, pos_owner, pos_row, neg_rows):
    examples, width = queries.shape
    table_rows = item_table.shape[0]
    neg_dev = neg_rows.shape[0]
    items = lax.axis_size("item")
    groups = lax.axis_size("dp")
    bits = groups.bit_length() - 1
    assert groups == 1 << bits and items % 2 == 0
    capacity = 3 * examples // items
    slots = -(-capacity // 128) * 128
    negs = groups * items * neg_dev
    item = lax.axis_index("item")

    own_gid = pos_owner[:, 0] * table_rows + pos_row
    my_ids = item * table_rows + neg_rows
    id_pad = -(-neg_dev // 128) * 128
    ints = jnp.concatenate([own_gid, jnp.pad(my_ids, (0, id_pad - neg_dev))])
    all_ints = to_all(ints, "item", items)
    gids = all_ints[:, :examples]
    column_ids = all_ints[:, examples : examples + neg_dev].reshape(items * neg_dev)
    my_negs = unit_rows(item_table[neg_rows])[0].astype(BF16)
    column_negs = to_all(my_negs, "item", items).reshape(items * neg_dev, width)
    all_ids = to_all(column_ids, "dp", groups).reshape(negs)
    all_negs = to_all(column_negs, "dp", groups).reshape(negs, width)

    ring = [(index, (index + 2) % items) for index in range(items)]
    pair = flip("item", items, 0)
    steps, block = [], queries
    for step in range(items // 2):
        if step:
            block = lax.ppermute(block, "item", ring)
        other = lax.ppermute(block, "item", pair)
        steps.append((block, other, (item - 2 * step) % items, ((item ^ 1) - 2 * step) % items))

    found, rank, rid, place = pl.pallas_call(
        route_kernel,
        out_shape=(
            jax.ShapeDtypeStruct((items * slots, width), BF16),
            jax.ShapeDtypeStruct((items, examples), F32),
            jax.ShapeDtypeStruct((items, slots), F32),
            jax.ShapeDtypeStruct((1, examples), F32),
        ),
        in_specs=[pl.BlockSpec(memory_space=pltpu.SMEM), whole(), whole(), whole()],
        out_specs=(whole(), whole(), whole(), whole()),
        scratch_shapes=[pltpu.VMEM((table_rows, width), BF16)],
        name="route",
    )(item[None], gids, own_gid[None, :], item_table)
    back = lax.all_to_all(
        found.reshape(items, slots, width), "item", split_axis=0, concat_axis=0, tiled=True
    ).reshape(items * slots, width)

    local_ids = (all_ids - item * table_rows).astype(F32)[None, :]
    blocks = [block for step in steps for block in step[:2]]
    sources = [source for step in steps for source in step[2:]]
    count = len(blocks)
    pull, out_rid, neg_part = pl.pallas_call(
        lambda *refs: owner_kernel(count, True, *refs),
        out_shape=(
            jax.ShapeDtypeStruct((count * slots, width), BF16),
            jax.ShapeDtypeStruct((count, slots), F32),
            jax.ShapeDtypeStruct((negs, width), F32),
        ),
        in_specs=[pl.BlockSpec(memory_space=pltpu.SMEM)]
        + [pl.BlockSpec(memory_space=pl.ANY)] * count
        + [whole()] * 5,
        out_specs=(whole(), whole(), whole()),
        scratch_shapes=[
            pltpu.VMEM((count, examples, width), BF16),
            pltpu.VMEM((negs, 128), F32),
            pltpu.VMEM((negs, slots), F32),
            pltpu.SemaphoreType.DMA((count,)),
        ],
        name="owner",
    )(jnp.stack([item] + sources), *blocks, rank, rid, found, all_negs, local_ids)

    parts = (INV_TEMP * neg_part).astype(BF16).reshape(groups, items, neg_dev, width)
    parts = parts.transpose(1, 0, 2, 3).reshape(items, groups * neg_dev, width)
    parts = lax.all_to_all(parts, "item", split_axis=0, concat_axis=0, tiled=True)
    neg_sum = jnp.sum(parts.astype(F32), axis=0).astype(BF16)
    for bit in range(bits):
        got = lax.ppermute(neg_sum, "dp", flip("dp", groups, bit))
        neg_sum = (neg_sum.astype(F32) + got.astype(F32)).astype(BF16)
    neg_spots = lax.dynamic_slice_in_dim(
        local_ids.reshape(groups, items, neg_dev), item, 1, 1
    ).reshape(1, groups * neg_dev)

    chunk = math.gcd(table_rows, 512)
    dense = pl.pallas_call(
        lambda *refs: scatter_kernel(1, *refs),
        out_shape=jax.ShapeDtypeStruct((table_rows, width), BF16),
        grid=(table_rows // chunk,),
        in_specs=[whole()] * 2,
        out_specs=pl.BlockSpec((chunk, width), lambda step: (step, 0)),
        name="scatter",
    )(pull, out_rid)
    half = table_rows // 2
    summed = []
    for side in range(2):
        order = list(range(bits)) if side == 0 else list(range(bits))[::-1]
        value = dense[side * half : (side + 1) * half]
        for bit in order:
            value = halve(value, "dp", groups, bit)
        for bit in order[::-1]:
            value = double(value, "dp", groups, bit)
        summed.append(value)
    g_unit = jnp.concatenate(summed, axis=0)

    new_table, new_state = pl.pallas_call(
        update_kernel,
        out_shape=(
            jax.ShapeDtypeStruct((table_rows, width), F32),
            jax.ShapeDtypeStruct((1, table_rows), F32),
        ),
        grid=(table_rows // chunk,),
        in_specs=[
            pl.BlockSpec((chunk, width), lambda step: (step, 0)),
            pl.BlockSpec((1, chunk), lambda step: (0, step)),
            pl.BlockSpec((chunk, width), lambda step: (step, 0)),
            whole(),
            whole(),
        ],
        out_specs=(
            pl.BlockSpec((chunk, width), lambda step: (step, 0)),
            pl.BlockSpec((1, chunk), lambda step: (0, step)),
        ),
        name="update",
    )(item_table, adagrad_state[None, :], g_unit, neg_sum, neg_spots)

    part = math.gcd(examples, 256)
    query_grad, example_loss = pl.pallas_call(
        home_kernel,
        out_shape=(
            jax.ShapeDtypeStruct((examples, width), BF16),
            jax.ShapeDtypeStruct((1, examples), F32),
        ),
        grid=(examples // part,),
        in_specs=[
            pl.BlockSpec((part, width), lambda step: (step, 0)),
            pl.BlockSpec((1, part), lambda step: (0, step)),
            pl.BlockSpec((1, part), lambda step: (0, step)),
            whole(),
            whole(),
            whole(),
        ],
        out_specs=(
            pl.BlockSpec((part, width), lambda step: (step, 0)),
            pl.BlockSpec((1, part), lambda step: (0, step)),
        ),
        name="home",
    )(queries, place, own_gid.astype(F32)[None, :], back, all_negs, all_ids.astype(F32)[None, :])
    return (query_grad, example_loss.reshape(examples), new_table, new_state.reshape(table_rows))


def solution(mesh):
    placed = (
        P(("dp", "item"), None),
        P("item", None),
        P("item"),
        P(("dp", "item"), None),
        P(("dp", "item")),
        P(("dp", "item")),
    )
    return jax.shard_map(
        on_device,
        mesh=mesh,
        in_specs=placed,
        out_specs=(P(("dp", "item"), None), P(("dp", "item")), P("item", None), P("item")),
        check_vma=False,
    )
```

```python
import math

import jax
import jax.numpy as jnp
from jax import lax
from jax.experimental import pallas as pl
from jax.experimental.pallas import tpu as pltpu
from jax.sharding import PartitionSpec as P

INV_TEMP = 20.0
LEARN_RATE = 0.05
EPSILON = 1e-06
LOG2_E = math.log2(math.e)
F32 = jnp.float32
BF16 = jnp.bfloat16
NT = (((1,), (1,)), ((), ()))


def unit_rows(matrix):
    back_norm = 1.0 / jnp.sqrt(jnp.sum(matrix * matrix, axis=-1, keepdims=True) + EPSILON)
    return (matrix * back_norm, back_norm)


def iota(shape, axis):
    return lax.broadcasted_iota(jnp.int32, shape, axis).astype(F32)


def to_sub(row):
    return jnp.transpose(jnp.broadcast_to(row, (128, row.shape[1])))[:, :1]


def to_lane(col):
    return jnp.transpose(jnp.broadcast_to(col, (col.shape[0], 128)))[:1, :]


def one_hot(test):
    return jnp.where(test, 1.0, 0.0).astype(BF16)


def earlier_count(mask):
    total, step = mask, 1
    lane = lax.broadcasted_iota(jnp.int32, mask.shape, 1)
    while step < mask.shape[1]:
        total = total + jnp.where(lane >= step, pltpu.roll(total, step, axis=1), 0.0)
        step *= 2
    return total - mask


def rows_at(start, size):
    return pl.ds(pl.multiple_of(start * size, size), size)


def route_kernel(me_ref, gid_ref, own_ref, table_ref, found_ref, rank_ref, rid_ref, place_ref, send_ref):
    blocks, examples = gid_ref.shape
    table_rows = table_ref.shape[0]
    slots = rid_ref.shape[1]
    chunk = math.gcd(table_rows, 512)
    base = me_ref[0] * table_rows

    def normalize(step, carry):
        part = table_ref[rows_at(step, chunk), :]
        send_ref[rows_at(step, chunk), :] = unit_rows(part)[0].astype(BF16)
        return carry

    lax.fori_loop(0, table_rows // chunk, normalize, 0)
    local = gid_ref[...] - base
    mine = jnp.logical_and(local >= 0, local < table_rows)
    rank = earlier_count(jnp.where(mine, 1.0, 0.0))
    rank_ref[...] = jnp.where(mine, rank, -1.0)
    local = local.astype(F32)

    owner = lax.broadcasted_iota(jnp.int32, (blocks, examples), 0)
    own = own_ref[...]
    named = jnp.logical_and(own >= owner * table_rows, own < (owner + 1) * table_rows)
    count = earlier_count(jnp.where(named, 1.0, 0.0))
    spot = jnp.where(named, count + owner.astype(F32) * slots, 0.0)
    place_ref[...] = jnp.sum(spot, axis=0, keepdims=True)

    for block in range(blocks):
        chosen = iota((slots, examples), 0) == rank_ref[block : block + 1, :]
        wanted = jnp.sum(
            jnp.where(chosen, local[block : block + 1, :], 0.0), axis=1, keepdims=True
        )
        rid_ref[block : block + 1, :] = to_lane(wanted)

    def find(pair, carry):
        ids = [to_sub(rid_ref[pl.ds(2 * pair + core, 1), :]) for core in range(2)]
        pick = one_hot(jnp.concatenate(ids, axis=0) == iota((2 * slots, table_rows), 1))
        got = jnp.dot(pick, send_ref[...], preferred_element_type=F32)
        found_ref[rows_at(pair, 2 * slots), :] = got.astype(BF16)
        return carry

    lax.fori_loop(0, blocks // 2, find, 0)


def neg_ids(part):
    digits = part.astype(F32)
    return digits[:, :1] * 4096.0 + digits[:, 1:2] * 64.0 + digits[:, 2:3]


def owner_kernel(first, me_ref, *refs):
    queries, refs = refs[:2], refs[2:]
    rank_ref, rid_ref, found_any, negs_ref, refs = *refs[:4], refs[4:]
    if first:
        pull_ref, outrid_ref, neg_ref, ids_ref, refs = *refs[:4], refs[4:]
    else:
        prior_ref, pull_ref, outrid_ref, neg_ref, refs = *refs[:4], refs[4:]
    held, found, nsub, exps, copy_sem = refs
    slots = rid_ref.shape[1]
    examples, width = held.shape[1], held.shape[2]
    negs = negs_ref.shape[0]
    chunk = math.gcd(negs, 256)
    copies = []
    for spot in range(2):
        source = rows_at(me_ref[1 + spot], slots)
        there = found.at[spot * slots : (spot + 1) * slots]
        copies.append(pltpu.make_async_copy(found_any.at[source], there, copy_sem.at[2 + spot]))
        copies.append(pltpu.make_async_copy(queries[spot], held.at[spot], copy_sem.at[spot]))
    for copy in copies:
        copy.start()
    base = (me_ref[0] * me_ref[3]).astype(F32)
    nsub[...] = jnp.broadcast_to(neg_ids(negs_ref[:, width:]) - base, nsub.shape)
    if first:
        ids_ref[...] = jnp.transpose(nsub[...])[:1, :]
    ranks = [rank_ref[pl.ds(me_ref[1 + spot], 1), :] for spot in range(2)]
    rids = [rid_ref[pl.ds(me_ref[1 + spot], 1), :] for spot in range(2)]
    rid = jnp.concatenate(rids, axis=1)
    outrid_ref[...] = rid
    for copy in copies:
        copy.wait()
    picked = []
    for spot in range(2):
        pick = one_hot(iota((slots, examples), 0) == ranks[spot])
        picked.append(jnp.dot(pick, held[spot], preferred_element_type=F32))
    query_hat, _ = unit_rows(jnp.concatenate(picked, axis=0))
    query_send = query_hat.astype(BF16)
    s_pos = jnp.sum(query_send.astype(F32) * found[...].astype(F32), axis=1, keepdims=True)
    pos_exp = to_lane(jnp.exp(INV_TEMP * s_pos))
    total = pos_exp
    for step in range(negs // chunk):
        part = pl.ds(step * chunk, chunk)
        scores = lax.dot_general(
            negs_ref[part, :width], query_send, NT, preferred_element_type=F32
        )
        keep = nsub[part, :][:, :1] != rid
        some = jnp.where(keep, jnp.exp2(scores * (INV_TEMP * LOG2_E)), 0.0)
        exps[part, :] = some.astype(BF16)
        total = total + jnp.sum(some, axis=0, keepdims=True)
    scale = 1.0 / total
    scaled = (query_send.astype(F32) * to_sub(scale)).astype(BF16)
    for step in range(negs // chunk):
        part = pl.ds(step * chunk, chunk)
        more = jnp.dot(exps[part, :], scaled, preferred_element_type=F32)
        neg_ref[part, :] = more if first else prior_ref[part, :] + more
    p_pos = to_sub(pos_exp * scale)
    pull_ref[...] = (INV_TEMP * (p_pos - 1.0) * query_hat).astype(BF16)


def scatter_kernel(pieces, start_ref, *refs):
    pulls, rids, outs, held = refs[:pieces], refs[pieces : 2 * pieces], refs[2 * pieces : -1], refs[-1]
    size = pulls[0].shape[0]
    for piece, pull_ref in enumerate(pulls):
        held[piece * size : (piece + 1) * size, :] = pull_ref[...]
    ids = jnp.concatenate([rid_ref[...] for rid_ref in rids], axis=1)
    for side, out_ref in enumerate(outs):
        rows = math.gcd(out_ref.shape[0], 512)
        for step in range(out_ref.shape[0] // rows):
            offset = (start_ref[side] + step * rows).astype(F32)
            put = one_hot(iota((rows, ids.shape[1]), 0) == ids - offset)
            part = jnp.dot(put, held[...], preferred_element_type=F32)
            out_ref[step * rows : (step + 1) * rows, :] = part.astype(BF16)


def home_kernel(me_ref, query_ref, place_ref, gid_ref, back_ref, negs_ref, ids_ref, grad_ref, loss_ref):
    examples, width = query_ref.shape
    spots = back_ref.shape[0]
    pick = one_hot(iota((examples, spots), 1) == to_sub(place_ref[...]))
    pos_e = jnp.dot(pick, back_ref[...], preferred_element_type=F32)
    query_hat, back_norm = unit_rows(query_ref[...].astype(F32))
    query_send = query_hat.astype(BF16)
    s_pos = INV_TEMP * jnp.sum(query_send.astype(F32) * pos_e, axis=1, keepdims=True)
    pos_exp = jnp.exp(s_pos)
    negs = negs_ref[:, :width]
    scores = lax.dot_general(query_send, negs, NT, preferred_element_type=F32)
    local = (gid_ref[...] - me_ref[0] * me_ref[1]).astype(F32)
    keep = ids_ref[...] != to_sub(local)
    part = jnp.where(keep, jnp.exp2(scores * (INV_TEMP * LOG2_E)), 0.0)
    total = pos_exp + jnp.sum(part, axis=1, keepdims=True)
    scale = 1.0 / total
    loss_ref[...] = to_lane(jnp.log(total) - s_pos)
    probs = (part * scale).astype(BF16)
    g_query = INV_TEMP * (
        (pos_exp * scale - 1.0) * pos_e + jnp.dot(probs, negs, preferred_element_type=F32)
    )
    along = jnp.sum(query_hat * g_query, axis=1, keepdims=True)
    grad_ref[...] = ((g_query - query_hat * along) * back_norm).astype(BF16)


def update_kernel(start_ref, table_ref, state_ref, *refs):
    pieces, refs = refs[:-6], refs[-6:]
    neg_ref, row_ref, new_ref, new_state_ref, held, copy_sem = refs
    rows = table_ref.shape[0]
    step = pl.program_id(0)

    @pl.when(step == 0)
    def _():
        size = pieces[0].shape[0]
        copies = [
            pltpu.make_async_copy(
                piece,
                held.at[pl.ds(pl.multiple_of(start_ref[spot], size), size)],
                copy_sem.at[spot],
            )
            for spot, piece in enumerate(pieces)
        ]
        for copy in copies:
            copy.start()
        for copy in copies:
            copy.wait()

    offset = (step * rows).astype(F32)
    put = one_hot(iota((rows, row_ref.shape[1]), 0) == row_ref[...] - offset)
    g_unit = held[rows_at(step, rows), :].astype(F32) + jnp.dot(
        put, neg_ref[...], preferred_element_type=F32
    )
    table = table_ref[...]
    unit, back_norm = unit_rows(table)
    g_row = (g_unit - unit * jnp.sum(unit * g_unit, axis=1, keepdims=True)) * back_norm
    state = to_sub(state_ref[...]) + jnp.mean(g_row * g_row, axis=1, keepdims=True)
    new_state_ref[...] = to_lane(state)
    new_ref[...] = table - g_row * (LEARN_RATE * lax.rsqrt(state))


def whole(ndim=2):
    return pl.BlockSpec(memory_space=pltpu.VMEM)


def flip(name, count, bit):
    return [(index, index ^ (1 << bit)) for index in range(count)]


def add(left, right):
    return (left.astype(F32) + right.astype(F32)).astype(BF16)


def halve(value, name, count, bit):
    half = value.shape[0] // 2
    mine = (lax.axis_index(name) >> bit) & 1
    give = lax.dynamic_slice_in_dim(value, (1 - mine) * half, half, 0)
    keep = lax.dynamic_slice_in_dim(value, mine * half, half, 0)
    return add(keep, lax.ppermute(give, name, flip(name, count, bit)))


def double(value, name, count, bit):
    mine = (lax.axis_index(name) >> bit) & 1
    got = lax.ppermute(value, name, flip(name, count, bit))
    low = jnp.concatenate([value, got], axis=0)
    high = jnp.concatenate([got, value], axis=0)
    return jnp.where(mine == 0, low, high)


def to_all(value, name, count):
    copies = jnp.broadcast_to(value[None], (count, *value.shape))
    return lax.all_to_all(copies, name, split_axis=0, concat_axis=0, tiled=True)


def cost(flops, traffic):
    return pl.CostEstimate(flops=int(flops), bytes_accessed=int(traffic), transcendentals=0)


def on_device(queries, item_table, adagrad_state, pos_owner, pos_row, neg_rows):
    examples, width = queries.shape
    table_rows = item_table.shape[0]
    neg_dev = neg_rows.shape[0]
    items = lax.axis_size("item")
    groups = lax.axis_size("dp")
    bits = groups.bit_length() - 1
    assert groups == 1 << bits and bits > 0
    assert items & (items - 1) == 0 and items > 1
    capacity = 3 * examples // items
    slots = -(-capacity // 128) * 128
    negs = groups * items * neg_dev
    item = lax.axis_index("item")
    group = lax.axis_index("dp")
    smem = pl.BlockSpec(memory_space=pltpu.SMEM)
    anywhere = pl.BlockSpec(memory_space=pl.ANY)

    ring = [(index, (index + 2) % items) for index in range(items)]
    pair = flip("item", items, 0)
    steps, block = [], queries
    for step in range(items // 2):
        if step:
            with jax.named_scope(f"ring{step}"):
                block = lax.ppermute(block, "item", ring)
        with jax.named_scope(f"pair{step}"):
            other = lax.ppermute(block, "item", pair)
        steps.append((block, other, (item - 2 * step) % items, ((item ^ 1) - 2 * step) % items))

    own_gid = pos_owner[:, 0] * table_rows + pos_row
    with jax.named_scope("gids"):
        gids = to_all(own_gid, "item", items)
    my_ids = item * table_rows + neg_rows
    digits = jnp.stack([my_ids // 4096, my_ids // 64 % 64, my_ids % 64], axis=1).astype(BF16)
    my_negs = unit_rows(item_table[neg_rows])[0].astype(BF16)
    my_negs = jnp.concatenate([my_negs, jnp.pad(digits, ((0, 0), (0, 125)))], axis=1)
    with jax.named_scope("negs_item"):
        column_negs = to_all(my_negs, "item", items).reshape(items * neg_dev, width + 128)
    with jax.named_scope("negs_dp"):
        all_negs = to_all(column_negs, "dp", groups).reshape(negs, width + 128)

    found, rank, rid, place = pl.pallas_call(
        route_kernel,
        out_shape=(
            jax.ShapeDtypeStruct((items * slots, width), BF16),
            jax.ShapeDtypeStruct((items, examples), F32),
            jax.ShapeDtypeStruct((items, slots), F32),
            jax.ShapeDtypeStruct((1, examples), F32),
        ),
        in_specs=[smem, whole(), whole(), whole()],
        out_specs=(whole(), whole(), whole(), whole()),
        scratch_shapes=[pltpu.VMEM((table_rows, width), BF16)],
        cost_estimate=cost(2 * items * slots * table_rows * width, 8 * table_rows * width),
        name="route",
    )(item[None], gids, own_gid[None, :], item_table)

    pulls, rids, neg_part = [], [], None
    for step, (block, other, source, other_source) in enumerate(steps):
        first = step == 0
        scalars = jnp.stack([item, source, other_source, jnp.int32(table_rows)])
        out = pl.pallas_call(
            lambda *refs, first=first: owner_kernel(first, *refs),
            out_shape=(
                jax.ShapeDtypeStruct((2 * slots, width), BF16),
                jax.ShapeDtypeStruct((1, 2 * slots), F32),
                jax.ShapeDtypeStruct((negs, width), F32),
            )
            + ((jax.ShapeDtypeStruct((1, negs), F32),) if first else ()),
            in_specs=[smem, anywhere, anywhere, whole(), whole(), anywhere, whole()]
            + ([] if first else [whole()]),
            out_specs=(whole(),) * (4 if first else 3),
            scratch_shapes=[
                pltpu.VMEM((2, examples, width), BF16),
                pltpu.VMEM((2 * slots, width), BF16),
                pltpu.VMEM((negs, 128), F32),
                pltpu.VMEM((negs, 2 * slots), BF16),
                pltpu.SemaphoreType.DMA((4,)),
            ],
            cost_estimate=cost(6 * slots * negs * width * 2, 8 * negs * width),
            name=f"owner{step}",
        )(
            *(scalars, block, other, rank, rid, found, all_negs),
            *(() if first else (neg_part,)),
        )
        pulls.append(out[0])
        rids.append(out[1])
        neg_part = out[2]
        if first:
            local_ids = out[3]

    with jax.named_scope("back"):
        back = lax.all_to_all(
            found.reshape(items, slots, width), "item", split_axis=0, concat_axis=0, tiled=True
        ).reshape(items * slots, width)

    quarter = table_rows // 4
    orders = [list(range(bits)), list(range(bits))[::-1]]
    firsts = [(group >> order[0]) & 1 for order in orders]
    starts = [2 * side * quarter for side in range(2)]

    def scatter(offsets, name):
        return pl.pallas_call(
            lambda *refs: scatter_kernel(len(pulls), *refs),
            out_shape=(jax.ShapeDtypeStruct((quarter, width), BF16),) * 2,
            in_specs=[smem] + [whole()] * (2 * len(pulls)),
            out_specs=(whole(), whole()),
            scratch_shapes=[pltpu.VMEM((items * slots, width), BF16)],
            cost_estimate=cost(4 * items * slots * quarter * width, 4 * quarter * width),
            name=name,
        )(jnp.stack(offsets), *pulls, *rids)

    gives = scatter([start + (1 - mine) * quarter for start, mine in zip(starts, firsts)], "give")
    gots = []
    for side in range(2):
        with jax.named_scope(f"halve{side}"):
            gots.append(
                lax.ppermute(gives[side], "dp", flip("dp", groups, orders[side][0]))
            )
    keeps = scatter([start + mine * quarter for start, mine in zip(starts, firsts)], "keep")
    pieces, places = [], []
    for side, order in enumerate(orders):
        value = add(keeps[side], gots[side])
        for bit in order[1:]:
            value = halve(value, "dp", groups, bit)
        for bit in order[:0:-1]:
            value = double(value, "dp", groups, bit)
        got = lax.ppermute(value, "dp", flip("dp", groups, order[0]))
        pieces += [value, got]
        places += [starts[side] + firsts[side] * quarter, starts[side] + (1 - firsts[side]) * quarter]

    neg_sum = (INV_TEMP * neg_part).astype(BF16).reshape(groups, items, neg_dev, width)
    for bit in range(items.bit_length() - 1):
        split = neg_sum.reshape(groups, neg_sum.shape[1] // 2, 2, neg_dev, width)
        mine = (item >> bit) & 1
        give = lax.dynamic_index_in_dim(split, 1 - mine, 2, keepdims=False)
        keep = lax.dynamic_index_in_dim(split, mine, 2, keepdims=False)
        neg_sum = add(keep, lax.ppermute(give, "item", flip("item", items, bit)))
    neg_sum = neg_sum.reshape(groups * neg_dev, width)
    for bit in range(bits):
        neg_sum = add(neg_sum, lax.ppermute(neg_sum, "dp", flip("dp", groups, bit)))
    neg_spots = lax.dynamic_slice_in_dim(
        local_ids.reshape(groups, items, neg_dev), item, 1, 1
    ).reshape(1, groups * neg_dev)

    chunk = math.gcd(table_rows, 512)
    new_table, new_state = pl.pallas_call(
        update_kernel,
        out_shape=(
            jax.ShapeDtypeStruct((table_rows, width), F32),
            jax.ShapeDtypeStruct((1, table_rows), F32),
        ),
        grid=(table_rows // chunk,),
        in_specs=[
            smem,
            pl.BlockSpec((chunk, width), lambda step: (step, 0)),
            pl.BlockSpec((1, chunk), lambda step: (0, step)),
            *[anywhere] * len(pieces),
            whole(),
            whole(),
        ],
        out_specs=(
            pl.BlockSpec((chunk, width), lambda step: (step, 0)),
            pl.BlockSpec((1, chunk), lambda step: (0, step)),
        ),
        scratch_shapes=[
            pltpu.VMEM((table_rows, width), BF16),
            pltpu.SemaphoreType.DMA((len(pieces),)),
        ],
        cost_estimate=cost(8 * table_rows * width, 10 * table_rows * width),
        name="update",
    )(jnp.stack(places), item_table, adagrad_state[None, :], *pieces, neg_sum, neg_spots)

    part = math.gcd(examples, 256)
    query_grad, example_loss = pl.pallas_call(
        home_kernel,
        out_shape=(
            jax.ShapeDtypeStruct((examples, width), BF16),
            jax.ShapeDtypeStruct((1, examples), F32),
        ),
        grid=(examples // part,),
        in_specs=[
            smem,
            pl.BlockSpec((part, width), lambda step: (step, 0)),
            pl.BlockSpec((1, part), lambda step: (0, step)),
            pl.BlockSpec((1, part), lambda step: (0, step)),
            whole(),
            whole(),
            whole(),
        ],
        out_specs=(
            pl.BlockSpec((part, width), lambda step: (step, 0)),
            pl.BlockSpec((1, part), lambda step: (0, step)),
        ),
        cost_estimate=cost(4 * examples * (negs + items * slots) * width, 8 * negs * width),
        name="home",
    )(
        jnp.stack([item, jnp.int32(table_rows)]),
        *(queries, place, own_gid[None, :], back, all_negs, local_ids),
    )
    return (query_grad, example_loss.reshape(examples), new_table, new_state.reshape(table_rows))


def solution(mesh):
    placed = (
        P(("dp", "item"), None),
        P("item", None),
        P("item"),
        P(("dp", "item"), None),
        P(("dp", "item")),
        P(("dp", "item")),
    )
    return jax.shard_map(
        on_device,
        mesh=mesh,
        in_specs=placed,
        out_specs=(P(("dp", "item"), None), P(("dp", "item")), P("item", None), P("item")),
        check_vma=False,
    )
```

```python
import math

import jax
import jax.numpy as jnp
from jax import lax
from jax.experimental import pallas as pl
from jax.experimental.pallas import tpu as pltpu
from jax.sharding import PartitionSpec as P

INV_TEMP = 20.0
LEARN_RATE = 0.05
EPSILON = 1e-06
LOG2_E = math.log2(math.e)
F32 = jnp.float32
BF16 = jnp.bfloat16
NT = (((1,), (1,)), ((), ()))


def unit_rows(matrix):
    back_norm = 1.0 / jnp.sqrt(jnp.sum(matrix * matrix, axis=-1, keepdims=True) + EPSILON)
    return (matrix * back_norm, back_norm)


def iota(shape, axis):
    return lax.broadcasted_iota(jnp.int32, shape, axis).astype(F32)


def to_sub(row):
    return jnp.transpose(jnp.broadcast_to(row, (8, row.shape[1])))[:, :1]


def to_lane(col):
    return jnp.transpose(jnp.broadcast_to(col, (col.shape[0], 128)))[:1, :]


def one_hot(test):
    return jnp.where(test, 1.0, 0.0).astype(BF16)


def earlier_count(mask):
    total, step = mask, 1
    lane = lax.broadcasted_iota(jnp.int32, mask.shape, 1)
    while step < mask.shape[1]:
        total = total + jnp.where(lane >= step, pltpu.roll(total, step, axis=1), 0.0)
        step *= 2
    return total - mask


def rows_at(start, size):
    return pl.ds(pl.multiple_of(start * size, size), size)


def route_kernel(gid_ref, own_ref, rows_ref, rank_ref, rid_ref, place_ref):
    blocks, examples = gid_ref.shape
    slots = rid_ref.shape[1]
    table_rows = rows_ref[0]
    local = gid_ref[...] - lax.axis_index("item") * table_rows
    mine = jnp.logical_and(local >= 0, local < table_rows)
    rank = earlier_count(jnp.where(mine, 1.0, 0.0))
    rank_ref[...] = jnp.where(mine, rank, -1.0)
    local = local.astype(F32)

    owner = lax.broadcasted_iota(jnp.int32, (blocks, examples), 0)
    own = own_ref[...]
    named = jnp.logical_and(own >= owner * table_rows, own < (owner + 1) * table_rows)
    count = earlier_count(jnp.where(named, 1.0, 0.0))
    spot = jnp.where(named, count + owner.astype(F32) * slots, 0.0)
    place_ref[...] = jnp.sum(spot, axis=0, keepdims=True)

    for block in range(blocks):
        chosen = iota((slots, examples), 0) == rank_ref[block : block + 1, :]
        wanted = jnp.sum(
            jnp.where(chosen, local[block : block + 1, :], 0.0), axis=1, keepdims=True
        )
        rid_ref[block : block + 1, :] = to_lane(wanted).astype(jnp.int32)


def norm_kernel(table_ref, send_ref):
    send_ref[...] = unit_rows(table_ref[...])[0].astype(BF16)


def find_kernel(start, rid_ref, send_ref, *refs):
    found_ref = refs[-1]
    table_rows = send_ref.shape[0]
    first = 2 * (start + pl.program_id(0))
    ids = [to_sub(rid_ref[pl.ds(first + core, 1), :].astype(F32)) for core in range(2)]
    pick = one_hot(jnp.concatenate(ids, axis=0) == iota((1, table_rows), 1))
    found_ref[...] = jnp.dot(pick, send_ref[...], preferred_element_type=F32).astype(BF16)


def neg_ids(part):
    digits = part.astype(F32)
    return digits[:, :1] * 4096.0 + digits[:, 1:2] * 64.0 + digits[:, 2:3]


def ring_source(spot, items):
    item = lax.axis_index("item")
    return lax.rem((item ^ (spot % 2)) - 2 * (spot // 2) + items, items)


def owner_kernel(table_rows, *refs):
    pairs, groups = lax.axis_size("item") // 2, lax.axis_size("dp")
    queries, refs = refs[: 2 * pairs], refs[2 * pairs :]
    columns, refs = refs[:groups], refs[groups:]
    rank_ref, rid_ref, found_any, refs = *refs[:3], refs[3:]
    pull_ref, outrid_ref, part_ref, ids_ref, negs_ref, refs = *refs[:5], refs[5:]
    held, found, nsub, exps, neg_ref, copy_sem = refs
    slots = rid_ref.shape[1]
    examples, width = held.shape[1], held.shape[2]
    negs = negs_ref.shape[0]
    chunk = math.gcd(negs, 256)
    both = 2 * slots
    size = negs // groups
    copies = [
        pltpu.make_async_copy(
            column,
            negs_ref.at[rows_at(lax.axis_index("dp") ^ other, size)],
            copy_sem.at[4 * pairs + other],
        )
        for other, column in enumerate(columns)
    ]
    for spot, query in enumerate(queries):
        source = rows_at(ring_source(spot, 2 * pairs), slots)
        there = found.at[spot * slots : (spot + 1) * slots]
        copies.append(
            pltpu.make_async_copy(query, held.at[spot], copy_sem.at[2 * spot + 1])
        )
        copies.append(
            pltpu.make_async_copy(found_any.at[source], there, copy_sem.at[2 * spot])
        )
    for copy in copies:
        copy.start()
    base = (lax.axis_index("item") * table_rows).astype(F32)
    for spot in range(2 * pairs):
        part = slice(spot * slots, (spot + 1) * slots)
        rid = rid_ref[pl.ds(ring_source(spot, 2 * pairs), 1), :]
        outrid_ref[:, part] = rid.astype(F32)
    for copy in copies:
        copy.wait()
    nsub[...] = jnp.broadcast_to(neg_ids(negs_ref[:, width:]) - base, nsub.shape)
    ids_ref[...] = jnp.transpose(nsub[...])[:1, :]

    def one_pair(pair, fresh):
        rid = outrid_ref[:, rows_at(pair, both)]
        picked = []
        for core in range(2):
            rank = rank_ref[pl.ds(ring_source(2 * pair + core, 2 * pairs), 1), :]
            pick = one_hot(iota((slots, examples), 0) == rank)
            picked.append(jnp.dot(pick, held[2 * pair + core], preferred_element_type=F32))
        query_hat, _ = unit_rows(jnp.concatenate(picked, axis=0))
        query_send = query_hat.astype(BF16)
        pos_e = found[rows_at(pair, both), :].astype(F32)
        s_pos = jnp.sum(query_send.astype(F32) * pos_e, axis=1, keepdims=True)
        pos_exp = to_lane(jnp.exp(INV_TEMP * s_pos))
        total = pos_exp
        for step in range(negs // chunk):
            part = pl.ds(step * chunk, chunk)
            scores = lax.dot_general(
                negs_ref[part, :width], query_send, NT, preferred_element_type=F32
            )
            keep = nsub[part, :][:, :1] != rid
            some = jnp.where(keep, jnp.exp2(scores * (INV_TEMP * LOG2_E)), 0.0)
            exps[part, :] = some.astype(BF16)
            total = total + jnp.sum(some, axis=0, keepdims=True)
        scale = 1.0 / total
        scaled = (query_send.astype(F32) * to_sub(scale)).astype(BF16)
        for step in range(negs // chunk):
            part = pl.ds(step * chunk, chunk)
            more = jnp.dot(exps[part, :], scaled, preferred_element_type=F32)
            if fresh:
                neg_ref[part, :] = more
            else:
                neg_ref[part, :] += more
        p_pos = to_sub(pos_exp * scale)
        pull = (INV_TEMP * (p_pos - 1.0) * query_hat).astype(BF16)
        pull_ref[rows_at(pair, both), :] = pull

    one_pair(0, True)
    if pairs > 1:

        def more_pairs(pair, carry):
            one_pair(pair, False)
            return carry

        lax.fori_loop(1, pairs, more_pairs, 0)
    part_ref[...] = (INV_TEMP * neg_ref[...]).astype(BF16)


def scatter_kernel(keep, bits, pull_ref, rid_ref, *outs):
    ids = rid_ref[...]
    for side, out_ref in enumerate(outs):
        quarter = out_ref.shape[0]
        rows = math.gcd(quarter, 512)
        mine = (lax.axis_index("dp") >> bits[side]) & 1
        start = (2 * side + (mine if keep else 1 - mine)) * quarter
        for step in range(out_ref.shape[0] // rows):
            offset = (start + step * rows).astype(F32)
            put = one_hot(iota((rows, ids.shape[1]), 0) == ids - offset)
            part = jnp.dot(put, pull_ref[...], preferred_element_type=F32)
            out_ref[step * rows : (step + 1) * rows, :] = part.astype(BF16)


def home_kernel(table_rows, query_ref, place_ref, gid_ref, back_ref, negs_ref, ids_ref, *refs):
    grad_ref, loss_ref = refs[-2:]
    examples, width = query_ref.shape
    spots = back_ref.shape[0]
    pick = one_hot(iota((examples, spots), 1) == to_sub(place_ref[...]))
    pos_e = jnp.dot(pick, back_ref[...], preferred_element_type=F32)
    query_hat, back_norm = unit_rows(query_ref[...].astype(F32))
    query_send = query_hat.astype(BF16)
    s_pos = INV_TEMP * jnp.sum(query_send.astype(F32) * pos_e, axis=1, keepdims=True)
    pos_exp = jnp.exp(s_pos)
    negs = negs_ref[:, :width]
    scores = lax.dot_general(query_send, negs, NT, preferred_element_type=F32)
    local = (gid_ref[...] - lax.axis_index("item") * table_rows).astype(F32)
    keep = ids_ref[...] != to_sub(local)
    part = jnp.where(keep, jnp.exp2(scores * (INV_TEMP * LOG2_E)), 0.0)
    total = pos_exp + jnp.sum(part, axis=1, keepdims=True)
    scale = 1.0 / total
    loss_ref[...] = to_lane(jnp.log(total) - s_pos)
    probs = (part * scale).astype(BF16)
    g_query = INV_TEMP * (
        (pos_exp * scale - 1.0) * pos_e + jnp.dot(probs, negs, preferred_element_type=F32)
    )
    along = jnp.sum(query_hat * g_query, axis=1, keepdims=True)
    grad_ref[...] = ((g_query - query_hat * along) * back_norm).astype(BF16)


def update_kernel(rest, start_ref, table_ref, state_ref, *refs):
    low_ref, high_ref, neg_ref, row_ref = refs[:4]
    new_ref, new_state_ref = refs[-2:]
    rows = table_ref.shape[0]
    step = pl.program_id(0)
    half = pl.num_programs(0) // 2
    offset = (update_block(rest, step, start_ref, half) * rows).astype(F32)
    put = one_hot(iota((rows, row_ref.shape[1]), 0) == row_ref[...] - offset)
    pull = jnp.where(step < half, low_ref[...].astype(F32), high_ref[...].astype(F32))
    g_unit = pull + jnp.dot(put, neg_ref[...], preferred_element_type=F32)
    table = table_ref[...]
    unit, back_norm = unit_rows(table)
    g_row = (g_unit - unit * jnp.sum(unit * g_unit, axis=1, keepdims=True)) * back_norm
    state = to_sub(state_ref[...]) + jnp.mean(g_row * g_row, axis=1, keepdims=True)
    new_state_ref[...] = to_lane(state)
    new_ref[...] = table - g_row * (LEARN_RATE * lax.rsqrt(state))


def update_block(rest, step, start_ref, half):
    low, high = start_ref[2 * rest], start_ref[2 * rest + 1]
    return jnp.where(step < half, low + step, high + step - half)


def whole():
    return pl.BlockSpec(memory_space=pltpu.VMEM)


def flip(count, bit):
    return [(index, index ^ (1 << bit)) for index in range(count)]


def add(left, right):
    return (left.astype(F32) + right.astype(F32)).astype(BF16)


def halve(value, name, count, bit):
    half = value.shape[0] // 2
    mine = (lax.axis_index(name) >> bit) & 1
    give = lax.dynamic_slice_in_dim(value, (1 - mine) * half, half, 0)
    keep = lax.dynamic_slice_in_dim(value, mine * half, half, 0)
    return add(keep, lax.ppermute(give, name, flip(count, bit)))


def double(value, name, count, bit):
    mine = (lax.axis_index(name) >> bit) & 1
    got = lax.ppermute(value, name, flip(count, bit))
    low = jnp.concatenate([value, got], axis=0)
    high = jnp.concatenate([got, value], axis=0)
    return jnp.where(mine == 0, low, high)


def to_digits(values, axis):
    digits = [values // 4096, values // 64 % 64, values % 64]
    return jnp.concatenate(digits, axis=axis).astype(BF16)


def to_all(value, name, count):
    copies = jnp.broadcast_to(value[None], (count, *value.shape))
    return lax.all_to_all(copies, name, split_axis=0, concat_axis=0, tiled=True)


def cost(flops, traffic):
    return pl.CostEstimate(flops=int(flops), bytes_accessed=int(traffic), transcendentals=0)


def on_device(queries, item_table, adagrad_state, pos_owner, pos_row, neg_rows):
    examples, width = queries.shape
    table_rows = item_table.shape[0]
    neg_dev = neg_rows.shape[0]
    items = lax.axis_size("item")
    groups = lax.axis_size("dp")
    bits = groups.bit_length() - 1
    assert groups == 1 << bits and bits > 0
    assert items & (items - 1) == 0 and items > 1
    capacity = 3 * examples // items
    slots = -(-capacity // 128) * 128
    negs = groups * items * neg_dev
    item = lax.axis_index("item")
    group = lax.axis_index("dp")
    smem = pl.BlockSpec(memory_space=pltpu.SMEM)
    anywhere = pl.BlockSpec(memory_space=pl.ANY)

    ring = [(index, (index + 2) % items) for index in range(items)]
    pair = flip(items, 0)
    steps, block = [], queries
    for step in range(items // 2):
        if step:
            block = lax.ppermute(block, "item", ring)
        other = lax.ppermute(block, "item", pair)
        steps.append((block, other))

    own_gid = pos_owner[:, 0] * table_rows + pos_row
    my_ids = item * table_rows + neg_rows
    lanes = -(-3 * examples // neg_dev)
    side_width = -(-(64 + lanes) // 128) * 128
    spread = jnp.pad(to_digits(own_gid, 0), (0, lanes * neg_dev - 3 * examples))
    payload = jnp.concatenate(
        [
            unit_rows(item_table[neg_rows])[0].astype(BF16),
            jnp.pad(to_digits(my_ids[:, None], 1), ((0, 0), (0, side_width - 3 - lanes))),
            spread.reshape(neg_dev, lanes),
        ],
        axis=1,
    )
    column = to_all(payload, "item", items)
    spread = column[:, :, width + side_width - lanes :].astype(jnp.int32)
    spread = spread.reshape(items, neg_dev * lanes)[:, : 3 * examples]
    spread = spread.reshape(items, 3, examples)
    gids = spread[:, 0] * 4096 + spread[:, 1] * 64 + spread[:, 2]
    column_negs = [column.reshape(items * neg_dev, width + side_width)]
    for other in range(1, groups):
        column_negs.append(
            lax.ppermute(column_negs[0], "dp", [(at, at ^ other) for at in range(groups)])
        )

    rank, rid, place = pl.pallas_call(
        route_kernel,
        out_shape=(
            jax.ShapeDtypeStruct((items, examples), F32),
            jax.ShapeDtypeStruct((items, slots), jnp.int32),
            jax.ShapeDtypeStruct((1, examples), F32),
        ),
        in_specs=[whole(), whole(), smem],
        out_specs=(whole(), whole(), whole()),
        cost_estimate=cost(2**32, 6 * table_rows * width),
        name="route",
    )(gids, own_gid[None, :], jnp.full((1,), table_rows, jnp.int32))
    chunk = math.gcd(table_rows, 512)
    tall = pl.BlockSpec((chunk, width), lambda step: (step, 0))
    send = pl.pallas_call(
        norm_kernel,
        out_shape=jax.ShapeDtypeStruct((table_rows, width), BF16),
        grid=(table_rows // chunk,),
        in_specs=[tall],
        out_specs=tall,
        cost_estimate=cost(2**32, 6 * table_rows * width),
        name="norm",
    )(item_table)
    found = ()
    for side in range(2):
        start = side * items // 4
        found = (
            pl.pallas_call(
                lambda *refs, start=start: find_kernel(start, *refs),
                out_shape=jax.ShapeDtypeStruct((items * slots, width), BF16),
                grid=(items // 4,),
                in_specs=[whole(), whole()] + [anywhere] * len(found),
                out_specs=pl.BlockSpec(
                    (2 * slots, width), lambda step, start=start: (start + step, 0)
                ),
                input_output_aliases={2: 0} if found else {},
                cost_estimate=cost(2**32, 8 * table_rows * width),
            )(rid, send, *found),
        )
    found = found[0]

    blocks = [block for step in steps for block in step]
    pull, out_rid, neg_part, local_ids, all_negs = pl.pallas_call(
        lambda *refs: owner_kernel(table_rows, *refs),
        out_shape=(
            jax.ShapeDtypeStruct((items * slots, width), BF16),
            jax.ShapeDtypeStruct((1, items * slots), F32),
            jax.ShapeDtypeStruct((negs, width), BF16),
            jax.ShapeDtypeStruct((1, negs), F32),
            jax.ShapeDtypeStruct((negs, width + side_width), BF16),
        ),
        in_specs=[anywhere] * (items + groups) + [whole(), whole(), anywhere],
        out_specs=(whole(),) * 5,
        scratch_shapes=[
            pltpu.VMEM((items, examples, width), BF16),
            pltpu.VMEM((items * slots, width), BF16),
            pltpu.VMEM((negs, 128), F32),
            pltpu.VMEM((negs, 2 * slots), BF16),
            pltpu.VMEM((negs, width), F32),
            pltpu.SemaphoreType.DMA((2 * items + groups,)),
        ],
        cost_estimate=cost(8 * items * slots * negs * width, 8 * negs * width),
        name="owner",
    )(*blocks, *column_negs, rank, rid, found)
    back = lax.all_to_all(
        found.reshape(items, slots, width), "item", split_axis=0, concat_axis=0, tiled=True
    ).reshape(items * slots, width)

    quarter = table_rows // 4
    orders = [list(range(bits)), list(range(bits))[::-1]]
    firsts = [(group >> order[0]) & 1 for order in orders]
    starts = [2 * side * quarter for side in range(2)]

    def scatter(keep):
        bits_used = [order[0] for order in orders]
        return pl.pallas_call(
            lambda *refs: scatter_kernel(keep, bits_used, *refs),
            out_shape=(jax.ShapeDtypeStruct((quarter, width), BF16),) * 2,
            in_specs=[whole(), whole()],
            out_specs=(whole(), whole()),
            cost_estimate=cost(4 * items * slots * quarter * width, 4 * quarter * width),
            name="keep" if keep else "give",
        )(pull, out_rid)

    gives = scatter(False)
    gots = []
    for side in range(2):
        gots.append(lax.ppermute(gives[side], "dp", flip(groups, orders[side][0])))
    keeps = scatter(True)
    values, others = [], []
    for side, order in enumerate(orders):
        value = add(keeps[side], gots[side])
        for level in range(1, bits):
            value = halve(value, "dp", groups, order[level])
        for level in range(bits - 1, 0, -1):
            value = double(value, "dp", groups, order[level])
        values.append(value)
        others.append(lax.ppermute(value, "dp", flip(groups, order[0])))

    neg_sum = neg_part.reshape(groups, items, neg_dev, width)
    for bit in range(items.bit_length() - 1):
        split = neg_sum.reshape(groups, neg_sum.shape[1] // 2, 2, neg_dev, width)
        mine = (item >> bit) & 1
        give = lax.dynamic_index_in_dim(split, 1 - mine, 2, keepdims=False)
        keep = lax.dynamic_index_in_dim(split, mine, 2, keepdims=False)
        neg_sum = add(keep, lax.ppermute(give, "item", flip(items, bit)))
    neg_sum = neg_sum.reshape(groups * neg_dev, width)
    for bit in range(bits):
        neg_sum = add(neg_sum, lax.ppermute(neg_sum, "dp", flip(groups, bit)))
    neg_spots = lax.dynamic_slice_in_dim(
        local_ids.reshape(groups, items, neg_dev), item, 1, 1
    ).reshape(1, groups * neg_dev)

    chunk = math.gcd(quarter, 512)
    per = quarter // chunk
    updated = ()
    places = jnp.stack(
        [
            (start + (first ^ rest) * quarter) // chunk
            for rest in range(2)
            for start, first in zip(starts, firsts)
        ]
    )
    for rest, pieces in enumerate((values, others)):
        tall = pl.BlockSpec(
            (chunk, width), lambda step, at, rest=rest: (update_block(rest, step, at, per), 0)
        )
        flat = pl.BlockSpec(
            (1, chunk), lambda step, at, rest=rest: (0, update_block(rest, step, at, per))
        )
        updated = pl.pallas_call(
            lambda *refs, rest=rest: update_kernel(rest, *refs),
            out_shape=(
                jax.ShapeDtypeStruct((table_rows, width), F32),
                jax.ShapeDtypeStruct((1, table_rows), F32),
            ),
            grid_spec=pltpu.PrefetchScalarGridSpec(
                num_scalar_prefetch=1,
                grid=(2 * per,),
                in_specs=[
                    tall,
                    flat,
                    pl.BlockSpec((chunk, width), lambda step, _: (jnp.minimum(step, per - 1), 0)),
                    pl.BlockSpec((chunk, width), lambda step, _: (jnp.maximum(step - per, 0), 0)),
                    whole(),
                    whole(),
                    *[anywhere] * len(updated),
                ],
                out_specs=(tall, flat),
            ),
            input_output_aliases={7: 0, 8: 1} if updated else {},
            cost_estimate=cost(2**32, 5 * table_rows * width),
            name="update_rest" if rest else "update_own",
        )(places, item_table, adagrad_state[None, :], *pieces, neg_sum, neg_spots, *updated)
    new_table, new_state = updated

    part = math.gcd(examples // 2, 256)
    per = examples // 2 // part
    homes = ()
    for side in range(2):
        tall = pl.BlockSpec((part, width), lambda step, side=side: (side * per + step, 0))
        flat = pl.BlockSpec((1, part), lambda step, side=side: (0, side * per + step))
        homes = pl.pallas_call(
            lambda *refs: home_kernel(table_rows, *refs),
            out_shape=(
                jax.ShapeDtypeStruct((examples, width), BF16),
                jax.ShapeDtypeStruct((1, examples), F32),
            ),
            grid=(per,),
            in_specs=[tall, flat, flat, whole(), whole(), whole()] + [anywhere] * len(homes),
            out_specs=(tall, flat),
            input_output_aliases={6: 0, 7: 1} if homes else {},
            cost_estimate=cost(2**32, 8 * negs * width),
        )(queries, place, own_gid[None, :], back, all_negs, local_ids, *homes)
    query_grad, example_loss = homes
    return (query_grad, example_loss.reshape(examples), new_table, new_state.reshape(table_rows))


def solution(mesh):
    placed = (
        P(("dp", "item"), None),
        P("item", None),
        P("item"),
        P(("dp", "item"), None),
        P(("dp", "item")),
        P(("dp", "item")),
    )

    return jax.shard_map(
        on_device,
        mesh=mesh,
        in_specs=placed,
        out_specs=(P(("dp", "item"), None), P(("dp", "item")), P("item", None), P("item")),
        check_vma=False,
    )
```

```python
import math

import jax
import jax.numpy as jnp
from jax import lax
from jax.experimental import pallas as pl
from jax.experimental.pallas import tpu as pltpu
from jax.sharding import PartitionSpec as P

INV_TEMP = 20.0
LEARN_RATE = 0.05
EPSILON = 1e-06
LOG2_E = math.log2(math.e)
F32 = jnp.float32
BF16 = jnp.bfloat16
NT = (((1,), (1,)), ((), ()))


def unit_rows(matrix):
    back_norm = 1.0 / jnp.sqrt(jnp.sum(matrix * matrix, axis=-1, keepdims=True) + EPSILON)
    return (matrix * back_norm, back_norm)


def iota(shape, axis):
    return lax.broadcasted_iota(jnp.int32, shape, axis).astype(F32)


def to_sub(row):
    return jnp.transpose(jnp.broadcast_to(row, (8, row.shape[1])))[:, :1]


def to_lane(col):
    return jnp.transpose(jnp.broadcast_to(col, (col.shape[0], 128)))[:1, :]


def one_hot(test):
    return jnp.where(test, 1.0, 0.0).astype(BF16)


def earlier_count(mask):
    total, step = mask, 1
    lane = lax.broadcasted_iota(jnp.int32, mask.shape, 1)
    while step < mask.shape[1]:
        total = total + jnp.where(lane >= step, pltpu.roll(total, step, axis=1), 0.0)
        step *= 2
    return total - mask


def rows_at(start, size):
    return pl.ds(pl.multiple_of(start * size, size), size)


def route_kernel(gid_ref, own_ref, rows_ref, rank_ref, rid_ref, place_ref):
    blocks, examples = gid_ref.shape
    slots = rid_ref.shape[1]
    table_rows = rows_ref[0]
    local = gid_ref[...] - lax.axis_index("item") * table_rows
    mine = jnp.logical_and(local >= 0, local < table_rows)
    rank = earlier_count(jnp.where(mine, 1.0, 0.0))
    rank_ref[...] = jnp.where(mine, rank, -1.0)
    local = local.astype(F32)

    owner = lax.broadcasted_iota(jnp.int32, (blocks, examples), 0)
    own = own_ref[...]
    named = jnp.logical_and(own >= owner * table_rows, own < (owner + 1) * table_rows)
    count = earlier_count(jnp.where(named, 1.0, 0.0))
    spot = jnp.where(named, count + owner.astype(F32) * slots, 0.0)
    place_ref[...] = jnp.sum(spot, axis=0, keepdims=True)

    for block in range(blocks):
        chosen = iota((slots, examples), 0) == rank_ref[block : block + 1, :]
        wanted = jnp.sum(
            jnp.where(chosen, local[block : block + 1, :], 0.0), axis=1, keepdims=True
        )
        rid_ref[block : block + 1, :] = to_lane(wanted).astype(jnp.int32)


def norm_kernel(table_ref, send_ref):
    send_ref[...] = unit_rows(table_ref[...])[0].astype(BF16)


def find_kernel(start, rid_ref, send_ref, *refs):
    found_ref = refs[-1]
    table_rows = send_ref.shape[0]
    first = 2 * (start + pl.program_id(0))
    ids = [to_sub(rid_ref[pl.ds(first + core, 1), :].astype(F32)) for core in range(2)]
    pick = one_hot(jnp.concatenate(ids, axis=0) == iota((1, table_rows), 1))
    found_ref[...] = jnp.dot(pick, send_ref[...], preferred_element_type=F32).astype(BF16)


def neg_ids(part):
    digits = part.astype(F32)
    return digits[:, :1] * 4096.0 + digits[:, 1:2] * 64.0 + digits[:, 2:3]


def ring_source(spot, items):
    item = lax.axis_index("item")
    return lax.rem((item ^ (spot % 2)) - 2 * (spot // 2) + items, items)


def owner_kernel(table_rows, *refs):
    pairs, groups = lax.axis_size("item") // 2, lax.axis_size("dp")
    queries, refs = refs[: 2 * pairs], refs[2 * pairs :]
    columns, refs = refs[:groups], refs[groups:]
    rank_ref, rid_ref, found_any, refs = *refs[:3], refs[3:]
    pull_ref, outrid_ref, part_ref, ids_ref, negs_ref, refs = *refs[:5], refs[5:]
    held, found, nsub, exps, neg_ref, copy_sem = refs
    slots = rid_ref.shape[1]
    examples, width = held.shape[1], held.shape[2]
    negs = negs_ref.shape[0]
    chunk = math.gcd(negs, 256)
    both = 2 * slots
    size = negs // groups
    copies = [
        pltpu.make_async_copy(
            column,
            negs_ref.at[rows_at(lax.axis_index("dp") ^ other, size)],
            copy_sem.at[4 * pairs + other],
        )
        for other, column in enumerate(columns)
    ]
    for spot, query in enumerate(queries):
        source = rows_at(ring_source(spot, 2 * pairs), slots)
        there = found.at[spot * slots : (spot + 1) * slots]
        copies.append(
            pltpu.make_async_copy(query, held.at[spot], copy_sem.at[2 * spot + 1])
        )
        copies.append(
            pltpu.make_async_copy(found_any.at[source], there, copy_sem.at[2 * spot])
        )
    for copy in copies:
        copy.start()
    base = (lax.axis_index("item") * table_rows).astype(F32)
    for spot in range(2 * pairs):
        part = slice(spot * slots, (spot + 1) * slots)
        rid = rid_ref[pl.ds(ring_source(spot, 2 * pairs), 1), :]
        outrid_ref[:, part] = rid.astype(F32)
    for copy in copies:
        copy.wait()
    nsub[...] = jnp.broadcast_to(neg_ids(negs_ref[:, width:]) - base, nsub.shape)
    ids_ref[...] = jnp.transpose(nsub[...])[:1, :]

    def one_pair(pair, fresh):
        rid = outrid_ref[:, rows_at(pair, both)]
        picked = []
        for core in range(2):
            rank = rank_ref[pl.ds(ring_source(2 * pair + core, 2 * pairs), 1), :]
            pick = one_hot(iota((slots, examples), 0) == rank)
            picked.append(jnp.dot(pick, held[2 * pair + core], preferred_element_type=F32))
        query_hat, _ = unit_rows(jnp.concatenate(picked, axis=0))
        query_send = query_hat.astype(BF16)
        pos_e = found[rows_at(pair, both), :].astype(F32)
        s_pos = jnp.sum(query_send.astype(F32) * pos_e, axis=1, keepdims=True)
        pos_exp = to_lane(jnp.exp(INV_TEMP * s_pos))
        total = pos_exp
        for step in range(negs // chunk):
            part = pl.ds(step * chunk, chunk)
            scores = lax.dot_general(
                negs_ref[part, :width], query_send, NT, preferred_element_type=F32
            )
            keep = nsub[part, :][:, :1] != rid
            some = jnp.where(keep, jnp.exp2(scores * (INV_TEMP * LOG2_E)), 0.0)
            exps[part, :] = some.astype(BF16)
            total = total + jnp.sum(some, axis=0, keepdims=True)
        scale = 1.0 / total
        scaled = (query_send.astype(F32) * to_sub(scale)).astype(BF16)
        for step in range(negs // chunk):
            part = pl.ds(step * chunk, chunk)
            more = jnp.dot(exps[part, :], scaled, preferred_element_type=F32)
            if fresh:
                neg_ref[part, :] = more
            else:
                neg_ref[part, :] += more
        p_pos = to_sub(pos_exp * scale)
        pull = (INV_TEMP * (p_pos - 1.0) * query_hat).astype(BF16)
        pull_ref[rows_at(pair, both), :] = pull

    one_pair(0, True)
    if pairs > 1:

        def more_pairs(pair, carry):
            one_pair(pair, False)
            return carry

        lax.fori_loop(1, pairs, more_pairs, 0)
    part_ref[...] = (INV_TEMP * neg_ref[...]).astype(BF16)


def scatter_kernel(others, pull_ref, rid_ref, *outs):
    ids = rid_ref[...]
    for other, out_ref in zip(others, outs):
        rows = math.gcd(out_ref.shape[0], 512)
        start = (lax.axis_index("dp") ^ other) * out_ref.shape[0]
        for step in range(out_ref.shape[0] // rows):
            offset = (start + step * rows).astype(F32)
            put = one_hot(iota((rows, 1), 0) == ids - offset)
            part = jnp.dot(put, pull_ref[...], preferred_element_type=F32)
            out_ref[step * rows : (step + 1) * rows, :] = part.astype(BF16)


def home_kernel(table_rows, query_ref, place_ref, gid_ref, back_ref, negs_ref, ids_ref, *refs):
    grad_ref, loss_ref = refs[-2:]
    examples, width = query_ref.shape
    spots = back_ref.shape[0]
    pick = one_hot(iota((examples, spots), 1) == to_sub(place_ref[...]))
    pos_e = jnp.dot(pick, back_ref[...], preferred_element_type=F32)
    query_hat, back_norm = unit_rows(query_ref[...].astype(F32))
    query_send = query_hat.astype(BF16)
    s_pos = INV_TEMP * jnp.sum(query_send.astype(F32) * pos_e, axis=1, keepdims=True)
    pos_exp = jnp.exp(s_pos)
    negs = negs_ref[:, :width]
    scores = lax.dot_general(query_send, negs, NT, preferred_element_type=F32)
    local = (gid_ref[...] - lax.axis_index("item") * table_rows).astype(F32)
    keep = ids_ref[...] != to_sub(local)
    part = jnp.where(keep, jnp.exp2(scores * (INV_TEMP * LOG2_E)), 0.0)
    total = pos_exp + jnp.sum(part, axis=1, keepdims=True)
    scale = 1.0 / total
    loss_ref[...] = to_lane(jnp.log(total) - s_pos)
    probs = (part * scale).astype(BF16)
    g_query = INV_TEMP * (
        (pos_exp * scale - 1.0) * pos_e + jnp.dot(probs, negs, preferred_element_type=F32)
    )
    along = jnp.sum(query_hat * g_query, axis=1, keepdims=True)
    grad_ref[...] = ((g_query - query_hat * along) * back_norm).astype(BF16)


def update_kernel(first, count, place_ref, table_ref, state_ref, *refs):
    pieces, refs = refs[:count], refs[count:]
    neg_ref, row_ref, new_ref, new_state_ref = *refs[:2], *refs[-2:]
    rows = table_ref.shape[0]
    step = pl.program_id(0)
    per = pl.num_programs(0) // count
    offset = (update_block(first, per, step, place_ref) * rows).astype(F32)
    put = one_hot(iota((rows, 1), 0) == row_ref[...] - offset)
    g_unit = pieces[0][...].astype(F32)
    for spot in range(1, count):
        g_unit = jnp.where(step >= spot * per, pieces[spot][...].astype(F32), g_unit)
    g_unit = g_unit + jnp.dot(put, neg_ref[...], preferred_element_type=F32)
    table = table_ref[...]
    unit, back_norm = unit_rows(table)
    g_row = (g_unit - unit * jnp.sum(unit * g_unit, axis=1, keepdims=True)) * back_norm
    state = to_sub(state_ref[...]) + jnp.mean(g_row * g_row, axis=1, keepdims=True)
    new_state_ref[...] = to_lane(state)
    new_ref[...] = table - g_row * (LEARN_RATE * lax.rsqrt(state))


def update_block(first, per, step, place_ref):
    return place_ref[first + step // per] + step % per


def whole():
    return pl.BlockSpec(memory_space=pltpu.VMEM)


def flip(count, bit):
    return [(index, index ^ (1 << bit)) for index in range(count)]


def add(left, right):
    return (left.astype(F32) + right.astype(F32)).astype(BF16)


def add(left, right):
    return (left.astype(F32) + right.astype(F32)).astype(BF16)


def to_digits(values, axis):
    digits = [values // 4096, values // 64 % 64, values % 64]
    return jnp.concatenate(digits, axis=axis).astype(BF16)


def to_all(value, name, count):
    copies = jnp.broadcast_to(value[None], (count, *value.shape))
    return lax.all_to_all(copies, name, split_axis=0, concat_axis=0, tiled=True)


def cost(flops, traffic):
    return pl.CostEstimate(flops=int(flops), bytes_accessed=int(traffic), transcendentals=0)


def on_device(queries, item_table, adagrad_state, pos_owner, pos_row, neg_rows):
    examples, width = queries.shape
    table_rows = item_table.shape[0]
    neg_dev = neg_rows.shape[0]
    items = lax.axis_size("item")
    groups = lax.axis_size("dp")
    assert groups & (groups - 1) == 0 and groups > 1
    assert items & (items - 1) == 0 and items > 1
    capacity = 3 * examples // items
    slots = -(-capacity // 128) * 128
    negs = groups * items * neg_dev
    item = lax.axis_index("item")
    group = lax.axis_index("dp")
    smem = pl.BlockSpec(memory_space=pltpu.SMEM)
    anywhere = pl.BlockSpec(memory_space=pl.ANY)

    ring = [(index, (index + 2) % items) for index in range(items)]
    pair = flip(items, 0)
    steps, block = [], queries
    for step in range(items // 2):
        if step:
            block = lax.ppermute(block, "item", ring)
        other = lax.ppermute(block, "item", pair)
        steps.append((block, other))

    own_gid = pos_owner[:, 0] * table_rows + pos_row
    my_ids = item * table_rows + neg_rows
    lanes = -(-3 * examples // neg_dev)
    side_width = -(-(64 + lanes) // 128) * 128
    spread = jnp.pad(to_digits(own_gid, 0), (0, lanes * neg_dev - 3 * examples))
    payload = jnp.concatenate(
        [
            unit_rows(item_table[neg_rows])[0].astype(BF16),
            jnp.pad(to_digits(my_ids[:, None], 1), ((0, 0), (0, side_width - 3 - lanes))),
            spread.reshape(neg_dev, lanes),
        ],
        axis=1,
    )
    column = to_all(payload, "item", items)
    spread = column[:, :, width + side_width - lanes :].astype(jnp.int32)
    spread = spread.reshape(items, neg_dev * lanes)[:, : 3 * examples]
    spread = spread.reshape(items, 3, examples)
    gids = spread[:, 0] * 4096 + spread[:, 1] * 64 + spread[:, 2]
    column_negs = [column.reshape(items * neg_dev, width + side_width)]
    for other in range(1, groups):
        column_negs.append(
            lax.ppermute(column_negs[0], "dp", [(at, at ^ other) for at in range(groups)])
        )

    rank, rid, place = pl.pallas_call(
        route_kernel,
        out_shape=(
            jax.ShapeDtypeStruct((items, examples), F32),
            jax.ShapeDtypeStruct((items, slots), jnp.int32),
            jax.ShapeDtypeStruct((1, examples), F32),
        ),
        in_specs=[whole(), whole(), smem],
        out_specs=(whole(), whole(), whole()),
        cost_estimate=cost(2**32, 6 * table_rows * width),
        name="route",
    )(gids, own_gid[None, :], jnp.full((1,), table_rows, jnp.int32))
    chunk = math.gcd(table_rows, 512)
    tall = pl.BlockSpec((chunk, width), lambda step: (step, 0))
    send = pl.pallas_call(
        norm_kernel,
        out_shape=jax.ShapeDtypeStruct((table_rows, width), BF16),
        grid=(table_rows // chunk,),
        in_specs=[tall],
        out_specs=tall,
        cost_estimate=cost(2**32, 6 * table_rows * width),
        name="norm",
    )(item_table)
    found = ()
    for start, count in ((0, 1), (1, items // 2 - 1)):
        found = (
            pl.pallas_call(
                lambda *refs, start=start: find_kernel(start, *refs),
                out_shape=jax.ShapeDtypeStruct((items * slots, width), BF16),
                grid=(count,),
                in_specs=[whole(), whole()] + [anywhere] * len(found),
                out_specs=pl.BlockSpec(
                    (2 * slots, width), lambda step, start=start: (start + step, 0)
                ),
                input_output_aliases={2: 0} if found else {},
                cost_estimate=cost(count * 2**31, 8 * table_rows * width),
            )(rid, send, *found),
        )
    found = found[0]

    blocks = [block for step in steps for block in step]
    pull, out_rid, neg_part, local_ids, all_negs = pl.pallas_call(
        lambda *refs: owner_kernel(table_rows, *refs),
        out_shape=(
            jax.ShapeDtypeStruct((items * slots, width), BF16),
            jax.ShapeDtypeStruct((1, items * slots), F32),
            jax.ShapeDtypeStruct((negs, width), BF16),
            jax.ShapeDtypeStruct((1, negs), F32),
            jax.ShapeDtypeStruct((negs, width + side_width), BF16),
        ),
        in_specs=[anywhere] * (items + groups) + [whole(), whole(), anywhere],
        out_specs=(whole(),) * 5,
        scratch_shapes=[
            pltpu.VMEM((items, examples, width), BF16),
            pltpu.VMEM((items * slots, width), BF16),
            pltpu.VMEM((negs, 128), F32),
            pltpu.VMEM((negs, 2 * slots), BF16),
            pltpu.VMEM((negs, width), F32),
            pltpu.SemaphoreType.DMA((2 * items + groups,)),
        ],
        cost_estimate=cost(8 * items * slots * negs * width, 8 * negs * width),
        name="owner",
    )(*blocks, *column_negs, rank, rid, found)
    back = lax.all_to_all(
        found.reshape(items, slots, width), "item", split_axis=0, concat_axis=0, tiled=True
    ).reshape(items * slots, width)

    assert table_rows % groups == 0
    quarter = table_rows // groups
    ways = [[(at, at ^ other) for at in range(groups)] for other in range(groups)]

    def scatter(others):
        return pl.pallas_call(
            lambda *refs: scatter_kernel(others, *refs),
            out_shape=(jax.ShapeDtypeStruct((quarter, width), BF16),) * len(others),
            in_specs=[whole(), whole()],
            out_specs=(whole(),) * len(others),
            cost_estimate=cost(
                2 * len(others) * items * slots * quarter * width, 4 * quarter * width
            ),
        )(pull, out_rid)

    gots = []
    near, far = list(range(1, groups - 1)), [groups - 1, 0]
    gives = scatter(near) if near else ()
    for other, give in zip(near, gives):
        gots.append(lax.ppermute(give, "dp", ways[other]))
    give, total = scatter(far)
    gots.append(lax.ppermute(give, "dp", ways[groups - 1]))
    total = total.astype(F32)
    for got in gots:
        total = total + got.astype(F32)
    values = [total.astype(BF16)]
    for other in range(1, groups):
        values.append(lax.ppermute(values[0], "dp", ways[other]))

    neg_sum = neg_part.reshape(groups, items, neg_dev, width)
    for bit in range(items.bit_length() - 1):
        split = neg_sum.reshape(groups, neg_sum.shape[1] // 2, 2, neg_dev, width)
        mine = (item >> bit) & 1
        give = lax.dynamic_index_in_dim(split, 1 - mine, 2, keepdims=False)
        keep = lax.dynamic_index_in_dim(split, mine, 2, keepdims=False)
        neg_sum = add(keep, lax.ppermute(give, "item", flip(items, bit)))
    neg_sum = neg_sum.reshape(groups * neg_dev, width)
    neg_parts = [neg_sum]
    for other in range(1, groups):
        neg_parts.append(lax.ppermute(neg_sum, "dp", ways[other]))
    neg_parts = [part.astype(F32) for part in neg_parts]
    while len(neg_parts) > 1:
        neg_parts = [low + high for low, high in zip(neg_parts[::2], neg_parts[1::2])]
    neg_sum = neg_parts[0].astype(BF16)
    neg_spots = lax.dynamic_slice_in_dim(
        local_ids.reshape(groups, items, neg_dev), item, 1, 1
    ).reshape(1, groups * neg_dev)

    chunk = math.gcd(quarter, 512)
    per = quarter // chunk
    updated = ()
    places = jnp.stack([(group ^ other) * per for other in range(groups)])
    for first, last in ((0, 1), (1, groups - 1), (groups - 1, groups)):
        pieces = values[first:last]
        if not pieces:
            continue
        count = len(pieces)
        tall = pl.BlockSpec(
            (chunk, width), lambda step, at, first=first: (update_block(first, per, step, at), 0)
        )
        flat = pl.BlockSpec(
            (1, chunk), lambda step, at, first=first: (0, update_block(first, per, step, at))
        )
        updated = pl.pallas_call(
            lambda *refs, first=first, count=count: update_kernel(first, count, *refs),
            out_shape=(
                jax.ShapeDtypeStruct((table_rows, width), F32),
                jax.ShapeDtypeStruct((1, table_rows), F32),
            ),
            grid_spec=pltpu.PrefetchScalarGridSpec(
                num_scalar_prefetch=1,
                grid=(count * per,),
                in_specs=[tall, flat]
                + [
                    pl.BlockSpec(
                        (chunk, width),
                        lambda step, _, spot=spot: (jnp.clip(step - spot * per, 0, per - 1), 0),
                    )
                    for spot in range(count)
                ]
                + [whole(), whole()]
                + [anywhere] * len(updated),
                out_specs=(tall, flat),
            ),
            input_output_aliases={5 + count: 0, 6 + count: 1} if updated else {},
            cost_estimate=cost(2**32, 5 * table_rows * width),
        )(places, item_table, adagrad_state[None, :], *pieces, neg_sum, neg_spots, *updated)
    new_table, new_state = updated

    part = math.gcd(examples // 2, 256)
    per = examples // 2 // part
    homes = ()
    for side in range(2):
        tall = pl.BlockSpec((part, width), lambda step, side=side: (side * per + step, 0))
        flat = pl.BlockSpec((1, part), lambda step, side=side: (0, side * per + step))
        homes = pl.pallas_call(
            lambda *refs: home_kernel(table_rows, *refs),
            out_shape=(
                jax.ShapeDtypeStruct((examples, width), BF16),
                jax.ShapeDtypeStruct((1, examples), F32),
            ),
            grid=(per,),
            in_specs=[tall, flat, flat, whole(), whole(), whole()] + [anywhere] * len(homes),
            out_specs=(tall, flat),
            input_output_aliases={6: 0, 7: 1} if homes else {},
            cost_estimate=cost(2**32, 8 * negs * width),
        )(queries, place, own_gid[None, :], back, all_negs, local_ids, *homes)
    query_grad, example_loss = homes
    return (query_grad, example_loss.reshape(examples), new_table, new_state.reshape(table_rows))


def solution(mesh):
    placed = (
        P(("dp", "item"), None),
        P("item", None),
        P("item"),
        P(("dp", "item"), None),
        P(("dp", "item")),
        P(("dp", "item")),
    )

    return jax.shard_map(
        on_device,
        mesh=mesh,
        in_specs=placed,
        out_specs=(P(("dp", "item"), None), P(("dp", "item")), P("item", None), P("item")),
        check_vma=False,
    )
```

```python
import math

import jax
import jax.numpy as jnp
from jax import lax
from jax.experimental import pallas as pl
from jax.experimental.pallas import tpu as pltpu
from jax.sharding import PartitionSpec as P

INV_TEMP = 20.0
LEARN_RATE = 0.05
EPSILON = 1e-06
LOG2_E = math.log2(math.e)
F32 = jnp.float32
BF16 = jnp.bfloat16
NT = (((1,), (1,)), ((), ()))


def unit_rows(matrix):
    back_norm = lax.rsqrt(jnp.sum(matrix * matrix, axis=-1, keepdims=True) + EPSILON)
    return (matrix * back_norm, back_norm)


def iota(shape, axis):
    return lax.broadcasted_iota(jnp.int32, shape, axis).astype(F32)


def to_sub(row):
    return jnp.transpose(jnp.broadcast_to(row, (8, row.shape[1])))[:, :1]


def to_lane(col):
    return jnp.transpose(jnp.broadcast_to(col, (col.shape[0], 128)))[:1, :]


def one_hot(test):
    return jnp.where(test, 1.0, 0.0).astype(BF16)


def earlier_count(mask):
    total, step = mask, 1
    lane = lax.broadcasted_iota(jnp.int32, mask.shape, 1)
    while step < mask.shape[1]:
        total = total + jnp.where(lane >= step, pltpu.roll(total, step, axis=1), 0.0)
        step *= 2
    return total - mask


def rows_at(start, size):
    return pl.ds(pl.multiple_of(start * size, size), size)


def route_kernel(gid_ref, own_ref, rows_ref, rank_ref, rid_ref, place_ref):
    blocks, examples = gid_ref.shape
    slots = rid_ref.shape[1]
    table_rows = rows_ref[0]
    local = gid_ref[...] - lax.axis_index("item") * table_rows
    mine = jnp.logical_and(local >= 0, local < table_rows)
    rank = earlier_count(jnp.where(mine, 1.0, 0.0))
    rank_ref[...] = jnp.where(mine, rank, -1.0)
    local = local.astype(F32)

    owner = lax.broadcasted_iota(jnp.int32, (blocks, examples), 0)
    own = own_ref[...]
    named = jnp.logical_and(own >= owner * table_rows, own < (owner + 1) * table_rows)
    count = earlier_count(jnp.where(named, 1.0, 0.0))
    spot = jnp.where(named, count + owner.astype(F32) * slots, 0.0)
    place_ref[...] = jnp.sum(spot, axis=0, keepdims=True)

    for block in range(blocks):
        chosen = iota((slots, examples), 0) == rank_ref[block : block + 1, :]
        wanted = jnp.sum(
            jnp.where(chosen, local[block : block + 1, :], 0.0), axis=1, keepdims=True
        )
        rid_ref[block : block + 1, :] = to_lane(wanted).astype(jnp.int32)


def norm_kernel(table_ref, send_ref):
    send_ref[...] = unit_rows(table_ref[...])[0].astype(BF16)


def find_kernel(start, rid_ref, send_ref, *refs):
    found_ref = refs[-1]
    table_rows = send_ref.shape[0]
    first = 2 * (start + pl.program_id(0))
    ids = [to_sub(rid_ref[pl.ds(first + core, 1), :].astype(F32)) for core in range(2)]
    pick = one_hot(jnp.concatenate(ids, axis=0) == iota((1, table_rows), 1))
    found_ref[...] = jnp.dot(pick, send_ref[...], preferred_element_type=F32).astype(BF16)


def neg_ids(part):
    digits = part.astype(F32)
    return digits[:, :1] * 4096.0 + digits[:, 1:2] * 64.0 + digits[:, 2:3]


def ring_source(spot, items):
    item = lax.axis_index("item")
    return lax.rem((item ^ (spot % 2)) - 2 * (spot // 2) + items, items)


def owner_kernel(table_rows, *refs):
    pairs, groups = lax.axis_size("item") // 2, lax.axis_size("dp")
    queries, refs = refs[: 2 * pairs], refs[2 * pairs :]
    columns, refs = refs[:groups], refs[groups:]
    rank_ref, rid_ref, found_any, refs = *refs[:3], refs[3:]
    pull_ref, outrid_ref, part_ref, ids_ref, negs_ref, spots_ref, refs = *refs[:6], refs[6:]
    held, found, nsub, exps, neg_ref, copy_sem = refs
    slots = rid_ref.shape[1]
    examples, width = held.shape[1], held.shape[2]
    negs = negs_ref.shape[0]
    chunk = math.gcd(negs, 768)
    both = 2 * slots
    size = negs // groups
    copies = [
        pltpu.make_async_copy(
            column,
            negs_ref.at[rows_at(lax.axis_index("dp") ^ other, size)],
            copy_sem.at[4 * pairs + other],
        )
        for other, column in enumerate(columns)
    ]
    for spot, query in enumerate(queries):
        source = rows_at(ring_source(spot, 2 * pairs), slots)
        there = found.at[spot * slots : (spot + 1) * slots]
        copies.append(
            pltpu.make_async_copy(query, held.at[spot], copy_sem.at[2 * spot + 1])
        )
        copies.append(
            pltpu.make_async_copy(found_any.at[source], there, copy_sem.at[2 * spot])
        )
    for copy in copies:
        copy.start()
    base = (lax.axis_index("item") * table_rows).astype(F32)
    for spot in range(2 * pairs):
        part = slice(spot * slots, (spot + 1) * slots)
        rid = rid_ref[pl.ds(ring_source(spot, 2 * pairs), 1), :]
        outrid_ref[:, part] = rid.astype(F32)
    for copy in copies:
        copy.wait()
    nsub[...] = jnp.broadcast_to(neg_ids(negs_ref[:, width:]) - base, nsub.shape)
    ids_ref[...] = jnp.transpose(nsub[...])[:1, :]
    mine = negs // groups // (2 * pairs)
    own = [
        nsub[rows_at(group * 2 * pairs + lax.axis_index("item"), mine), :]
        for group in range(groups)
    ]
    spare = spots_ref.shape[1] - groups * mine
    if spare:
        own.append(jnp.full((spare, 128), -1.0, F32))
    spots_ref[...] = jnp.transpose(jnp.concatenate(own, axis=0))[:1, :]

    def one_pair(pair, fresh):
        rid = outrid_ref[:, rows_at(pair, both)]
        picked = []
        for core in range(2):
            rank = rank_ref[pl.ds(ring_source(2 * pair + core, 2 * pairs), 1), :]
            pick = one_hot(iota((slots, examples), 0) == rank)
            picked.append(jnp.dot(pick, held[2 * pair + core], preferred_element_type=F32))
        query_hat, _ = unit_rows(jnp.concatenate(picked, axis=0))
        query_send = query_hat.astype(BF16)
        pos_e = found[rows_at(pair, both), :].astype(F32)
        s_pos = jnp.sum(query_send.astype(F32) * pos_e, axis=1, keepdims=True)
        pos_exp = to_lane(jnp.exp(INV_TEMP * s_pos))
        total = pos_exp
        for step in range(negs // chunk):
            part = pl.ds(step * chunk, chunk)
            scores = lax.dot_general(
                negs_ref[part, :width], query_send, NT, preferred_element_type=F32
            )
            keep = nsub[part, :][:, :1] != rid
            some = jnp.where(keep, jnp.exp2(scores * (INV_TEMP * LOG2_E)), 0.0)
            exps[part, :] = some.astype(BF16)
            total = total + jnp.sum(some, axis=0, keepdims=True)
        scale = 1.0 / total
        scaled = (query_send.astype(F32) * to_sub(scale)).astype(BF16)
        for step in range(negs // chunk):
            part = pl.ds(step * chunk, chunk)
            more = jnp.dot(exps[part, :], scaled, preferred_element_type=F32)
            if fresh:
                neg_ref[part, :] = more
            else:
                neg_ref[part, :] += more
        p_pos = to_sub(pos_exp * scale)
        pull = (INV_TEMP * (p_pos - 1.0) * query_hat).astype(BF16)
        pull_ref[rows_at(pair, both), :] = pull

    one_pair(0, True)
    if pairs > 1:

        def more_pairs(pair, carry):
            one_pair(pair, False)
            return carry

        lax.fori_loop(1, pairs, more_pairs, 0)
    part_ref[...] = (INV_TEMP * neg_ref[...]).astype(BF16)


def scatter_kernel(others, pull_ref, rid_ref, *outs):
    ids = rid_ref[...]
    for other, out_ref in zip(others, outs):
        rows = math.gcd(out_ref.shape[0], 1024)
        start = (lax.axis_index("dp") ^ other) * out_ref.shape[0]
        for step in range(out_ref.shape[0] // rows):
            offset = (start + step * rows).astype(F32)
            put = one_hot(iota((rows, 1), 0) == ids - offset)
            part = jnp.dot(put, pull_ref[...], preferred_element_type=F32)
            out_ref[step * rows : (step + 1) * rows, :] = part.astype(BF16)


def home_kernel(table_rows, query_ref, place_ref, gid_ref, back_ref, negs_ref, ids_ref, *refs):
    grad_ref, loss_ref = refs[-2:]
    examples, width = query_ref.shape
    spots = back_ref.shape[0]
    pick = one_hot(iota((examples, spots), 1) == to_sub(place_ref[...]))
    pos_e = jnp.dot(pick, back_ref[...], preferred_element_type=F32)
    query_hat, back_norm = unit_rows(query_ref[...].astype(F32))
    query_send = query_hat.astype(BF16)
    s_pos = INV_TEMP * jnp.sum(query_send.astype(F32) * pos_e, axis=1, keepdims=True)
    pos_exp = jnp.exp(s_pos)
    negs = negs_ref[:, :width]
    scores = lax.dot_general(query_send, negs, NT, preferred_element_type=F32)
    local = (gid_ref[...] - lax.axis_index("item") * table_rows).astype(F32)
    keep = ids_ref[...] != to_sub(local)
    part = jnp.where(keep, jnp.exp2(scores * (INV_TEMP * LOG2_E)), 0.0)
    total = pos_exp + jnp.sum(part, axis=1, keepdims=True)
    scale = 1.0 / total
    loss_ref[...] = to_lane(jnp.log(total) - s_pos)
    probs = (part * scale).astype(BF16)
    g_query = INV_TEMP * (
        (pos_exp * scale - 1.0) * pos_e + jnp.dot(probs, negs, preferred_element_type=F32)
    )
    along = jnp.sum(query_hat * g_query, axis=1, keepdims=True)
    grad_ref[...] = ((g_query - query_hat * along) * back_norm).astype(BF16)


def update_kernel(first, count, place_ref, table_ref, state_ref, *refs):
    pieces, refs = refs[:count], refs[count:]
    neg_ref, row_ref, new_ref, new_state_ref = *refs[:2], *refs[-2:]
    rows = table_ref.shape[0]
    step = pl.program_id(0)
    per = pl.num_programs(0) // count
    offset = (update_block(first, per, step, place_ref) * rows).astype(F32)
    put = one_hot(iota((rows, 1), 0) == row_ref[:, : neg_ref.shape[0]] - offset)
    g_unit = pieces[0][...].astype(F32)
    for spot in range(1, count):
        g_unit = jnp.where(step >= spot * per, pieces[spot][...].astype(F32), g_unit)
    g_unit = g_unit + jnp.dot(put, neg_ref[...], preferred_element_type=F32)
    table = table_ref[...]
    unit, back_norm = unit_rows(table)
    g_row = (g_unit - unit * jnp.sum(unit * g_unit, axis=1, keepdims=True)) * back_norm
    state = to_sub(state_ref[...]) + jnp.mean(g_row * g_row, axis=1, keepdims=True)
    new_state_ref[...] = to_lane(state)
    new_ref[...] = table - g_row * (LEARN_RATE * lax.rsqrt(state))


def update_block(first, per, step, place_ref):
    return place_ref[first + step // per] + step % per


def whole():
    return pl.BlockSpec(memory_space=pltpu.VMEM)


def flip(count, bit):
    return [(index, index ^ (1 << bit)) for index in range(count)]


def add(left, right):
    return (left.astype(F32) + right.astype(F32)).astype(BF16)


def add(left, right):
    return (left.astype(F32) + right.astype(F32)).astype(BF16)


def to_digits(values, axis):
    digits = [values // 4096, values // 64 % 64, values % 64]
    return jnp.concatenate(digits, axis=axis).astype(BF16)


def to_all(value, name, count):
    copies = jnp.broadcast_to(value[None], (count, *value.shape))
    return lax.all_to_all(copies, name, split_axis=0, concat_axis=0, tiled=True)


def cost(flops, traffic):
    return pl.CostEstimate(flops=int(flops), bytes_accessed=int(traffic), transcendentals=0)


def on_device(queries, item_table, adagrad_state, pos_owner, pos_row, neg_rows):
    examples, width = queries.shape
    table_rows = item_table.shape[0]
    neg_dev = neg_rows.shape[0]
    items = lax.axis_size("item")
    groups = lax.axis_size("dp")
    assert groups & (groups - 1) == 0 and groups > 1
    assert items & (items - 1) == 0 and items > 1
    capacity = 3 * examples // items
    slots = -(-capacity // 128) * 128
    negs = groups * items * neg_dev
    item = lax.axis_index("item")
    group = lax.axis_index("dp")
    smem = pl.BlockSpec(memory_space=pltpu.SMEM)
    anywhere = pl.BlockSpec(memory_space=pl.ANY)

    ring = [(index, (index + 2) % items) for index in range(items)]
    pair = flip(items, 0)
    steps, block = [], queries
    for step in range(items // 2):
        if step:
            block = lax.ppermute(block, "item", ring)
        other = lax.ppermute(block, "item", pair)
        steps.append((block, other))

    own_gid = pos_owner[:, 0] * table_rows + pos_row
    my_ids = item * table_rows + neg_rows
    lanes = -(-3 * examples // neg_dev)
    side_width = -(-(64 + lanes) // 128) * 128
    spread = jnp.pad(to_digits(own_gid, 0), (0, lanes * neg_dev - 3 * examples))
    payload = jnp.concatenate(
        [
            unit_rows(item_table[neg_rows])[0].astype(BF16),
            jnp.pad(to_digits(my_ids[:, None], 1), ((0, 0), (0, side_width - 3 - lanes))),
            spread.reshape(neg_dev, lanes),
        ],
        axis=1,
    )
    column = to_all(payload, "item", items)
    spread = column[:, :, width + side_width - lanes :].astype(jnp.int32)
    spread = spread.reshape(items, neg_dev * lanes)[:, : 3 * examples]
    spread = spread.reshape(items, 3, examples)
    gids = spread[:, 0] * 4096 + spread[:, 1] * 64 + spread[:, 2]
    column_negs = [column.reshape(items * neg_dev, width + side_width)]
    for other in range(1, groups):
        column_negs.append(
            lax.ppermute(column_negs[0], "dp", [(at, at ^ other) for at in range(groups)])
        )

    rank, rid, place = pl.pallas_call(
        route_kernel,
        out_shape=(
            jax.ShapeDtypeStruct((items, examples), F32),
            jax.ShapeDtypeStruct((items, slots), jnp.int32),
            jax.ShapeDtypeStruct((1, examples), F32),
        ),
        in_specs=[whole(), whole(), smem],
        out_specs=(whole(), whole(), whole()),
        cost_estimate=cost(2**32, 6 * table_rows * width),
        name="route",
    )(gids, own_gid[None, :], jnp.full((1,), table_rows, jnp.int32))
    chunk = math.gcd(table_rows, 512)
    tall = pl.BlockSpec((chunk, width), lambda step: (step, 0))
    send = pl.pallas_call(
        norm_kernel,
        out_shape=jax.ShapeDtypeStruct((table_rows, width), BF16),
        grid=(table_rows // chunk,),
        in_specs=[tall],
        out_specs=tall,
        cost_estimate=cost(2**32, 6 * table_rows * width),
        name="norm",
    )(item_table)
    found = ()
    for start, count in ((0, 1), (1, items // 2 - 1)):
        found = (
            pl.pallas_call(
                lambda *refs, start=start: find_kernel(start, *refs),
                out_shape=jax.ShapeDtypeStruct((items * slots, width), BF16),
                grid=(count,),
                in_specs=[whole(), whole()] + [anywhere] * len(found),
                out_specs=pl.BlockSpec(
                    (2 * slots, width), lambda step, start=start: (start + step, 0)
                ),
                input_output_aliases={2: 0} if found else {},
                cost_estimate=cost(count * 2**31, 8 * table_rows * width),
            )(rid, send, *found),
        )
    found = found[0]

    blocks = [block for step in steps for block in step]
    pull, out_rid, neg_part, local_ids, all_negs, neg_spots = pl.pallas_call(
        lambda *refs: owner_kernel(table_rows, *refs),
        out_shape=(
            jax.ShapeDtypeStruct((items * slots, width), BF16),
            jax.ShapeDtypeStruct((1, items * slots), F32),
            jax.ShapeDtypeStruct((negs, width), BF16),
            jax.ShapeDtypeStruct((1, negs), F32),
            jax.ShapeDtypeStruct((negs, width + side_width), BF16),
            jax.ShapeDtypeStruct((1, -(-groups * neg_dev // 128) * 128), F32),
        ),
        in_specs=[anywhere] * (items + groups) + [whole(), whole(), anywhere],
        out_specs=(whole(),) * 6,
        scratch_shapes=[
            pltpu.VMEM((items, examples, width), BF16),
            pltpu.VMEM((items * slots, width), BF16),
            pltpu.VMEM((negs, 128), F32),
            pltpu.VMEM((negs, 2 * slots), BF16),
            pltpu.VMEM((negs, width), F32),
            pltpu.SemaphoreType.DMA((2 * items + groups,)),
        ],
        cost_estimate=cost(8 * items * slots * negs * width, 8 * negs * width),
        name="owner",
    )(*blocks, *column_negs, rank, rid, found)
    back = lax.all_to_all(
        found.reshape(items, slots, width), "item", split_axis=0, concat_axis=0, tiled=True
    ).reshape(items * slots, width)

    assert table_rows % groups == 0
    quarter = table_rows // groups
    ways = [[(at, at ^ other) for at in range(groups)] for other in range(groups)]

    def scatter(others):
        return pl.pallas_call(
            lambda *refs: scatter_kernel(others, *refs),
            out_shape=(jax.ShapeDtypeStruct((quarter, width), BF16),) * len(others),
            in_specs=[whole(), whole()],
            out_specs=(whole(),) * len(others),
            cost_estimate=cost(
                2 * len(others) * items * slots * quarter * width, 4 * quarter * width
            ),
        )(pull, out_rid)

    gots = []
    near, far = list(range(1, groups - 1)), [groups - 1, 0]
    gives = scatter(near) if near else ()
    for other, give in zip(near, gives):
        gots.append(lax.ppermute(give, "dp", ways[other]))
    give, total = scatter(far)
    gots.append(lax.ppermute(give, "dp", ways[groups - 1]))
    total = total.astype(F32)
    for got in gots:
        total = total + got.astype(F32)
    values = [total.astype(BF16)]
    for other in near:
        values.append(lax.ppermute(values[0], "dp", ways[other]))
    tails = []
    if near:
        middle = quarter // 2
        for other, half in ((near[0], slice(0, middle)), (near[-1], slice(middle, quarter))):
            tails.append(
                lax.ppermute(values[other][half], "dp", ways[(groups - 1) ^ other])
            )
    else:
        tails.append(lax.ppermute(values[0], "dp", ways[groups - 1]))

    neg_sum = neg_part.reshape(groups, items, neg_dev, width)
    for bit in range(items.bit_length() - 1):
        split = neg_sum.reshape(groups, neg_sum.shape[1] // 2, 2, neg_dev, width)
        mine = (item >> bit) & 1
        give = lax.dynamic_index_in_dim(split, 1 - mine, 2, keepdims=False)
        keep = lax.dynamic_index_in_dim(split, mine, 2, keepdims=False)
        neg_sum = add(keep, lax.ppermute(give, "item", flip(items, bit)))
    neg_sum = neg_sum.reshape(groups * neg_dev, width)
    neg_parts = [neg_sum]
    for other in range(1, groups):
        neg_parts.append(lax.ppermute(neg_sum, "dp", ways[other]))
    neg_parts = [part.astype(F32) for part in neg_parts]
    while len(neg_parts) > 1:
        neg_parts = [low + high for low, high in zip(neg_parts[::2], neg_parts[1::2])]
    neg_sum = neg_parts[0].astype(BF16)
    updated = ()
    size = quarter // len(tails)
    chunk = math.gcd(size, 512)
    places = [(group ^ other) * (quarter // chunk) for other in range(groups)]
    places += [places[-1] + part * (size // chunk) for part in range(1, len(tails))]
    places = jnp.stack(places)
    for first, pieces in ((0, values[:1]), (1, values[1:]), (groups - 1, tails)):
        if not pieces:
            continue
        count = len(pieces)
        per = pieces[0].shape[0] // chunk
        tall = pl.BlockSpec(
            (chunk, width), lambda step, at, first=first, per=per: (update_block(first, per, step, at), 0)
        )
        flat = pl.BlockSpec(
            (1, chunk), lambda step, at, first=first, per=per: (0, update_block(first, per, step, at))
        )
        updated = pl.pallas_call(
            lambda *refs, first=first, count=count: update_kernel(first, count, *refs),
            out_shape=(
                jax.ShapeDtypeStruct((table_rows, width), F32),
                jax.ShapeDtypeStruct((1, table_rows), F32),
            ),
            grid_spec=pltpu.PrefetchScalarGridSpec(
                num_scalar_prefetch=1,
                grid=(count * per,),
                in_specs=[tall, flat]
                + [
                    pl.BlockSpec(
                        (chunk, width),
                        lambda step, _, spot=spot, per=per: (
                            jnp.clip(step - spot * per, 0, per - 1),
                            0,
                        ),
                    )
                    for spot in range(count)
                ]
                + [whole(), whole()]
                + [anywhere] * len(updated),
                out_specs=(tall, flat),
            ),
            input_output_aliases={5 + count: 0, 6 + count: 1} if updated else {},
            cost_estimate=cost(2**32, 5 * table_rows * width),
        )(places, item_table, adagrad_state[None, :], *pieces, neg_sum, neg_spots, *updated)
    new_table, new_state = updated

    part = math.gcd(examples, 512)
    tall = pl.BlockSpec((part, width), lambda step: (step, 0))
    flat = pl.BlockSpec((1, part), lambda step: (0, step))
    query_grad, example_loss = pl.pallas_call(
        lambda *refs: home_kernel(table_rows, *refs),
        out_shape=(
            jax.ShapeDtypeStruct((examples, width), BF16),
            jax.ShapeDtypeStruct((1, examples), F32),
        ),
        grid=(examples // part,),
        in_specs=[tall, flat, flat, whole(), whole(), whole()],
        out_specs=(tall, flat),
        cost_estimate=cost(2**33, 8 * negs * width),
        name="home",
    )(queries, place, own_gid[None, :], back, all_negs, local_ids)
    return (query_grad, example_loss.reshape(examples), new_table, new_state.reshape(table_rows))


def solution(mesh):
    placed = (
        P(("dp", "item"), None),
        P("item", None),
        P("item"),
        P(("dp", "item"), None),
        P(("dp", "item")),
        P(("dp", "item")),
    )

    return jax.shard_map(
        on_device,
        mesh=mesh,
        in_specs=placed,
        out_specs=(P(("dp", "item"), None), P(("dp", "item")), P("item", None), P("item")),
        check_vma=False,
    )
```

```python
import math

import jax
import jax.numpy as jnp
from jax import lax
from jax.experimental import pallas as pl
from jax.experimental.pallas import tpu as pltpu
from jax.sharding import PartitionSpec as P

INV_TEMP = 20.0
LEARN_RATE = 0.05
EPSILON = 1e-06
LOG2_E = math.log2(math.e)
F32 = jnp.float32
BF16 = jnp.bfloat16
NT = (((1,), (1,)), ((), ()))


def unit_rows(matrix):
    back_norm = lax.rsqrt(jnp.sum(matrix * matrix, axis=-1, keepdims=True) + EPSILON)
    return (matrix * back_norm, back_norm)


def iota(shape, axis):
    return lax.broadcasted_iota(jnp.int32, shape, axis).astype(F32)


def to_sub(row):
    return jnp.transpose(jnp.broadcast_to(row, (8, row.shape[1])))[:, :1]


def to_lane(col):
    return jnp.transpose(jnp.broadcast_to(col, (col.shape[0], 128)))[:1, :]


def one_hot(test):
    return jnp.where(test, 1.0, 0.0).astype(BF16)


def earlier_count(mask):
    total, step = mask, 1
    lane = lax.broadcasted_iota(jnp.int32, mask.shape, 1)
    while step < mask.shape[1]:
        total = total + jnp.where(lane >= step, pltpu.roll(total, step, axis=1), 0.0)
        step *= 2
    return total - mask


def rows_at(start, size):
    return pl.ds(pl.multiple_of(start * size, size), size)


def route_kernel(gid_ref, own_ref, rows_ref, rank_ref, rid_ref, place_ref):
    blocks, examples = gid_ref.shape
    slots = rid_ref.shape[1]
    table_rows = rows_ref[0]
    local = gid_ref[...] - lax.axis_index("item") * table_rows
    mine = jnp.logical_and(local >= 0, local < table_rows)
    rank = earlier_count(jnp.where(mine, 1.0, 0.0))
    rank_ref[...] = jnp.where(mine, rank, -1.0)
    local = local.astype(F32)

    owner = lax.broadcasted_iota(jnp.int32, (blocks, examples), 0)
    own = own_ref[...]
    named = jnp.logical_and(own >= owner * table_rows, own < (owner + 1) * table_rows)
    count = earlier_count(jnp.where(named, 1.0, 0.0))
    spot = jnp.where(named, count + owner.astype(F32) * slots, 0.0)
    place_ref[...] = jnp.sum(spot, axis=0, keepdims=True)

    for block in range(blocks):
        chosen = iota((slots, examples), 0) == rank_ref[block : block + 1, :]
        wanted = jnp.sum(
            jnp.where(chosen, local[block : block + 1, :], 0.0), axis=1, keepdims=True
        )
        rid_ref[block : block + 1, :] = to_lane(wanted).astype(jnp.int32)


def norm_kernel(table_ref, send_ref):
    send_ref[...] = unit_rows(table_ref[...])[0].astype(BF16)


def find_kernel(start, rid_ref, send_ref, *refs):
    found_ref = refs[-1]
    table_rows = send_ref.shape[0]
    first = 2 * (start + pl.program_id(0))
    ids = [to_sub(rid_ref[pl.ds(first + core, 1), :].astype(F32)) for core in range(2)]
    pick = one_hot(jnp.concatenate(ids, axis=0) == iota((1, table_rows), 1))
    found_ref[...] = jnp.dot(pick, send_ref[...], preferred_element_type=F32).astype(BF16)


def neg_ids(part):
    digits = part.astype(F32)
    return digits[:, :1] * 4096.0 + digits[:, 1:2] * 64.0 + digits[:, 2:3]


def ring_source(spot, items):
    item = lax.axis_index("item")
    return lax.rem((item ^ (spot % 2)) - 2 * (spot // 2) + items, items)


def owner_kernel(table_rows, *refs):
    pairs, groups = lax.axis_size("item") // 2, lax.axis_size("dp")
    queries, refs = refs[: 2 * pairs], refs[2 * pairs :]
    columns, refs = refs[:groups], refs[groups:]
    rank_ref, rid_ref, found_any, refs = *refs[:3], refs[3:]
    pull_ref, outrid_ref, part_ref, ids_ref, negs_ref, spots_ref, refs = *refs[:6], refs[6:]
    held, found, nsub, exps, neg_ref, copy_sem = refs
    slots = rid_ref.shape[1]
    examples, width = held.shape[1], held.shape[2]
    negs = negs_ref.shape[0]
    chunk = math.gcd(negs, 768)
    both = 2 * slots
    size = negs // groups
    copies = [
        pltpu.make_async_copy(
            column,
            negs_ref.at[rows_at(lax.axis_index("dp") ^ other, size)],
            copy_sem.at[4 * pairs + other],
        )
        for other, column in enumerate(columns)
    ]
    for spot, query in enumerate(queries):
        source = rows_at(ring_source(spot, 2 * pairs), slots)
        there = found.at[spot * slots : (spot + 1) * slots]
        copies.append(
            pltpu.make_async_copy(query, held.at[spot], copy_sem.at[2 * spot + 1])
        )
        copies.append(
            pltpu.make_async_copy(found_any.at[source], there, copy_sem.at[2 * spot])
        )
    for copy in copies:
        copy.start()
    base = (lax.axis_index("item") * table_rows).astype(F32)
    for spot in range(2 * pairs):
        part = slice(spot * slots, (spot + 1) * slots)
        rid = rid_ref[pl.ds(ring_source(spot, 2 * pairs), 1), :]
        outrid_ref[:, part] = rid.astype(F32)
    for copy in copies:
        copy.wait()
    nsub[...] = jnp.broadcast_to(neg_ids(negs_ref[:, width:]) - base, nsub.shape)
    ids_ref[...] = jnp.transpose(nsub[...])[:1, :]
    mine = negs // groups // (2 * pairs)
    own = [
        nsub[rows_at(group * 2 * pairs + lax.axis_index("item"), mine), :]
        for group in range(groups)
    ]
    spare = spots_ref.shape[1] - groups * mine
    if spare:
        own.append(jnp.full((spare, 128), -1.0, F32))
    spots_ref[...] = jnp.transpose(jnp.concatenate(own, axis=0))[:1, :]

    def one_pair(pair, fresh):
        rid = outrid_ref[:, rows_at(pair, both)]
        picked = []
        for core in range(2):
            rank = rank_ref[pl.ds(ring_source(2 * pair + core, 2 * pairs), 1), :]
            pick = one_hot(iota((slots, examples), 0) == rank)
            picked.append(jnp.dot(pick, held[2 * pair + core], preferred_element_type=F32))
        query_hat, _ = unit_rows(jnp.concatenate(picked, axis=0))
        query_send = query_hat.astype(BF16)
        pos_e = found[rows_at(pair, both), :].astype(F32)
        s_pos = jnp.sum(query_send.astype(F32) * pos_e, axis=1, keepdims=True)
        pos_exp = to_lane(jnp.exp(INV_TEMP * s_pos))
        total = pos_exp
        for step in range(negs // chunk):
            part = pl.ds(step * chunk, chunk)
            scores = lax.dot_general(
                negs_ref[part, :width], query_send, NT, preferred_element_type=F32
            )
            keep = nsub[part, :][:, :1] != rid
            some = jnp.where(keep, jnp.exp2(scores * (INV_TEMP * LOG2_E)), 0.0)
            exps[part, :] = some.astype(BF16)
            total = total + jnp.sum(some, axis=0, keepdims=True)
        scale = 1.0 / total
        scaled = (query_send.astype(F32) * to_sub(scale)).astype(BF16)
        for step in range(negs // chunk):
            part = pl.ds(step * chunk, chunk)
            more = jnp.dot(exps[part, :], scaled, preferred_element_type=F32)
            if fresh:
                neg_ref[part, :] = more
            else:
                neg_ref[part, :] += more
        p_pos = to_sub(pos_exp * scale)
        pull = (INV_TEMP * (p_pos - 1.0) * query_hat).astype(BF16)
        pull_ref[rows_at(pair, both), :] = pull

    one_pair(0, True)
    if pairs > 1:

        def more_pairs(pair, carry):
            one_pair(pair, False)
            return carry

        lax.fori_loop(1, pairs, more_pairs, 0)
    part_ref[...] = (INV_TEMP * neg_ref[...]).astype(BF16)


def scatter_kernel(others, pull_ref, rid_ref, *outs):
    ids = rid_ref[...]
    for other, out_ref in zip(others, outs):
        rows = math.gcd(out_ref.shape[0], 1024)
        start = (lax.axis_index("dp") ^ other) * out_ref.shape[0]
        for step in range(out_ref.shape[0] // rows):
            offset = (start + step * rows).astype(F32)
            put = one_hot(iota((rows, 1), 0) == ids - offset)
            part = jnp.dot(put, pull_ref[...], preferred_element_type=F32)
            out_ref[step * rows : (step + 1) * rows, :] = part.astype(BF16)


def home_kernel(table_rows, query_ref, place_ref, gid_ref, back_ref, negs_ref, ids_ref, *refs):
    grad_ref, loss_ref = refs[-2:]
    examples, width = query_ref.shape
    spots = back_ref.shape[0]
    pick = one_hot(iota((examples, spots), 1) == to_sub(place_ref[...]))
    pos_e = jnp.dot(pick, back_ref[...], preferred_element_type=F32)
    query_hat, back_norm = unit_rows(query_ref[...].astype(F32))
    query_send = query_hat.astype(BF16)
    s_pos = INV_TEMP * jnp.sum(query_send.astype(F32) * pos_e, axis=1, keepdims=True)
    pos_exp = jnp.exp(s_pos)
    negs = negs_ref[:, :width]
    scores = lax.dot_general(query_send, negs, NT, preferred_element_type=F32)
    local = (gid_ref[...] - lax.axis_index("item") * table_rows).astype(F32)
    keep = ids_ref[...] != to_sub(local)
    part = jnp.where(keep, jnp.exp2(scores * (INV_TEMP * LOG2_E)), 0.0)
    total = pos_exp + jnp.sum(part, axis=1, keepdims=True)
    scale = 1.0 / total
    loss_ref[...] = to_lane(jnp.log(total) - s_pos)
    probs = (part * scale).astype(BF16)
    g_query = INV_TEMP * (
        (pos_exp * scale - 1.0) * pos_e + jnp.dot(probs, negs, preferred_element_type=F32)
    )
    along = jnp.sum(query_hat * g_query, axis=1, keepdims=True)
    grad_ref[...] = ((g_query - query_hat * along) * back_norm).astype(BF16)


def update_kernel(first, count, place_ref, table_ref, state_ref, *refs):
    pieces, refs = refs[:count], refs[count:]
    neg_ref, row_ref, new_ref, new_state_ref = *refs[:2], *refs[-2:]
    rows = table_ref.shape[0]
    step = pl.program_id(0)
    per = pl.num_programs(0) // count
    offset = (update_block(first, per, step, place_ref) * rows).astype(F32)
    put = one_hot(iota((rows, 1), 0) == row_ref[:, : neg_ref.shape[0]] - offset)
    g_unit = pieces[0][...].astype(F32)
    for spot in range(1, count):
        g_unit = jnp.where(step >= spot * per, pieces[spot][...].astype(F32), g_unit)
    g_unit = g_unit + jnp.dot(put, neg_ref[...], preferred_element_type=F32)
    table = table_ref[...]
    unit, back_norm = unit_rows(table)
    g_row = (g_unit - unit * jnp.sum(unit * g_unit, axis=1, keepdims=True)) * back_norm
    state = to_sub(state_ref[...]) + jnp.mean(g_row * g_row, axis=1, keepdims=True)
    new_state_ref[...] = to_lane(state)
    new_ref[...] = table - g_row * (LEARN_RATE * lax.rsqrt(state))


def update_block(first, per, step, place_ref):
    return place_ref[first + step // per] + step % per


def whole():
    return pl.BlockSpec(memory_space=pltpu.VMEM)


def flip(count, bit):
    return [(index, index ^ (1 << bit)) for index in range(count)]


def add(left, right):
    return (left.astype(F32) + right.astype(F32)).astype(BF16)


def add(left, right):
    return (left.astype(F32) + right.astype(F32)).astype(BF16)


def to_digits(values, axis):
    digits = [values // 4096, values // 64 % 64, values % 64]
    return jnp.concatenate(digits, axis=axis).astype(BF16)


def to_all(value, name, count):
    copies = jnp.broadcast_to(value[None], (count, *value.shape))
    return lax.all_to_all(copies, name, split_axis=0, concat_axis=0, tiled=True)


def cost(flops, traffic):
    return pl.CostEstimate(flops=int(flops), bytes_accessed=int(traffic), transcendentals=0)


def on_device(queries, item_table, adagrad_state, pos_owner, pos_row, neg_rows):
    examples, width = queries.shape
    table_rows = item_table.shape[0]
    neg_dev = neg_rows.shape[0]
    items = lax.axis_size("item")
    groups = lax.axis_size("dp")
    assert groups & (groups - 1) == 0 and groups > 1
    assert items & (items - 1) == 0 and items > 1
    capacity = 3 * examples // items
    slots = -(-capacity // 128) * 128
    negs = groups * items * neg_dev
    item = lax.axis_index("item")
    group = lax.axis_index("dp")
    smem = pl.BlockSpec(memory_space=pltpu.SMEM)
    anywhere = pl.BlockSpec(memory_space=pl.ANY)

    ring = [(index, (index + 2) % items) for index in range(items)]
    pair = flip(items, 0)
    steps, block = [], queries
    for step in range(items // 2):
        if step:
            block = lax.ppermute(block, "item", ring)
        other = lax.ppermute(block, "item", pair)
        steps.append((block, other))

    own_gid = pos_owner[:, 0] * table_rows + pos_row
    my_ids = item * table_rows + neg_rows
    lanes = -(-3 * examples // neg_dev)
    side_width = -(-(64 + lanes) // 128) * 128
    spread = jnp.pad(to_digits(own_gid, 0), (0, lanes * neg_dev - 3 * examples))
    payload = jnp.concatenate(
        [
            unit_rows(item_table[neg_rows])[0].astype(BF16),
            jnp.pad(to_digits(my_ids[:, None], 1), ((0, 0), (0, side_width - 3 - lanes))),
            spread.reshape(neg_dev, lanes),
        ],
        axis=1,
    )
    column = to_all(payload, "item", items)
    spread = column[:, :, width + side_width - lanes :].astype(jnp.int32)
    spread = spread.reshape(items, neg_dev * lanes)[:, : 3 * examples]
    spread = spread.reshape(items, 3, examples)
    gids = spread[:, 0] * 4096 + spread[:, 1] * 64 + spread[:, 2]
    column_negs = [column.reshape(items * neg_dev, width + side_width)]
    for other in range(1, groups):
        column_negs.append(
            lax.ppermute(column_negs[0], "dp", [(at, at ^ other) for at in range(groups)])
        )

    rank, rid, place = pl.pallas_call(
        route_kernel,
        out_shape=(
            jax.ShapeDtypeStruct((items, examples), F32),
            jax.ShapeDtypeStruct((items, slots), jnp.int32),
            jax.ShapeDtypeStruct((1, examples), F32),
        ),
        in_specs=[whole(), whole(), smem],
        out_specs=(whole(), whole(), whole()),
        cost_estimate=cost(2**32, 6 * table_rows * width),
        name="route",
    )(gids, own_gid[None, :], jnp.full((1,), table_rows, jnp.int32))
    chunk = math.gcd(table_rows, 512)
    tall = pl.BlockSpec((chunk, width), lambda step: (step, 0))
    send = pl.pallas_call(
        norm_kernel,
        out_shape=jax.ShapeDtypeStruct((table_rows, width), BF16),
        grid=(table_rows // chunk,),
        in_specs=[tall],
        out_specs=tall,
        cost_estimate=cost(2**32, 6 * table_rows * width),
        name="norm",
    )(item_table)
    found = ()
    for start, count in ((0, 1), (1, items // 2 - 1)):
        found = (
            pl.pallas_call(
                lambda *refs, start=start: find_kernel(start, *refs),
                out_shape=jax.ShapeDtypeStruct((items * slots, width), BF16),
                grid=(count,),
                in_specs=[whole(), whole()] + [anywhere] * len(found),
                out_specs=pl.BlockSpec(
                    (2 * slots, width), lambda step, start=start: (start + step, 0)
                ),
                input_output_aliases={2: 0} if found else {},
                cost_estimate=cost(count * 2**31, 8 * table_rows * width),
            )(rid, send, *found),
        )
    found = found[0]

    blocks = [block for step in steps for block in step]
    pull, out_rid, neg_part, local_ids, all_negs, neg_spots = pl.pallas_call(
        lambda *refs: owner_kernel(table_rows, *refs),
        out_shape=(
            jax.ShapeDtypeStruct((items * slots, width), BF16),
            jax.ShapeDtypeStruct((1, items * slots), F32),
            jax.ShapeDtypeStruct((negs, width), BF16),
            jax.ShapeDtypeStruct((1, negs), F32),
            jax.ShapeDtypeStruct((negs, width + side_width), BF16),
            jax.ShapeDtypeStruct((1, -(-groups * neg_dev // 128) * 128), F32),
        ),
        in_specs=[anywhere] * (items + groups) + [whole(), whole(), anywhere],
        out_specs=(whole(),) * 6,
        scratch_shapes=[
            pltpu.VMEM((items, examples, width), BF16),
            pltpu.VMEM((items * slots, width), BF16),
            pltpu.VMEM((negs, 128), F32),
            pltpu.VMEM((negs, 2 * slots), BF16),
            pltpu.VMEM((negs, width), F32),
            pltpu.SemaphoreType.DMA((2 * items + groups,)),
        ],
        cost_estimate=cost(8 * items * slots * negs * width, 8 * negs * width),
        name="owner",
    )(*blocks, *column_negs, rank, rid, found)
    back = lax.all_to_all(
        found.reshape(items, slots, width), "item", split_axis=0, concat_axis=0, tiled=True
    ).reshape(items * slots, width)

    assert table_rows % groups == 0
    quarter = table_rows // groups
    ways = [[(at, at ^ other) for at in range(groups)] for other in range(groups)]

    def scatter(others):
        return pl.pallas_call(
            lambda *refs: scatter_kernel(others, *refs),
            out_shape=(jax.ShapeDtypeStruct((quarter, width), BF16),) * len(others),
            in_specs=[whole(), whole()],
            out_specs=(whole(),) * len(others),
            cost_estimate=cost(
                2 * len(others) * items * slots * quarter * width, 4 * quarter * width
            ),
        )(pull, out_rid)

    gots = []
    near, far = list(range(1, groups - 1)), [groups - 1, 0]
    gives = scatter(near) if near else ()
    for other, give in zip(near, gives):
        gots.append(lax.ppermute(give, "dp", ways[other]))
    give, total = scatter(far)
    gots.append(lax.ppermute(give, "dp", ways[groups - 1]))
    total = total.astype(F32)
    for got in gots:
        total = total + got.astype(F32)
    values = [total.astype(BF16)]
    for other in near:
        values.append(lax.ppermute(values[0], "dp", ways[other]))
    tails = []
    if near:
        middle = quarter // 2
        for other, half in ((near[0], slice(0, middle)), (near[-1], slice(middle, quarter))):
            tails.append(
                lax.ppermute(values[other][half], "dp", ways[(groups - 1) ^ other])
            )
    else:
        tails.append(lax.ppermute(values[0], "dp", ways[groups - 1]))

    neg_sum = neg_part.reshape(groups, items, neg_dev, width)
    for bit in range(items.bit_length() - 1):
        split = neg_sum.reshape(groups, neg_sum.shape[1] // 2, 2, neg_dev, width)
        mine = (item >> bit) & 1
        give = lax.dynamic_index_in_dim(split, 1 - mine, 2, keepdims=False)
        keep = lax.dynamic_index_in_dim(split, mine, 2, keepdims=False)
        neg_sum = add(keep, lax.ppermute(give, "item", flip(items, bit)))
    neg_sum = neg_sum.reshape(groups * neg_dev, width)
    neg_parts = [neg_sum]
    for other in range(1, groups):
        neg_parts.append(lax.ppermute(neg_sum, "dp", ways[other]))
    neg_parts = [part.astype(F32) for part in neg_parts]
    while len(neg_parts) > 1:
        neg_parts = [low + high for low, high in zip(neg_parts[::2], neg_parts[1::2])]
    neg_sum = neg_parts[0].astype(BF16)
    updated = ()
    size = quarter // len(tails)
    chunk = math.gcd(size, 512)
    places = [(group ^ other) * (quarter // chunk) for other in range(groups)]
    places += [places[-1] + part * (size // chunk) for part in range(1, len(tails))]
    places = jnp.stack(places)
    for first, pieces in ((0, values[:1]), (1, values[1:]), (groups - 1, tails)):
        if not pieces:
            continue
        count = len(pieces)
        per = pieces[0].shape[0] // chunk
        tall = pl.BlockSpec(
            (chunk, width), lambda step, at, first=first, per=per: (update_block(first, per, step, at), 0)
        )
        flat = pl.BlockSpec(
            (1, chunk), lambda step, at, first=first, per=per: (0, update_block(first, per, step, at))
        )
        updated = pl.pallas_call(
            lambda *refs, first=first, count=count: update_kernel(first, count, *refs),
            out_shape=(
                jax.ShapeDtypeStruct((table_rows, width), F32),
                jax.ShapeDtypeStruct((1, table_rows), F32),
            ),
            grid_spec=pltpu.PrefetchScalarGridSpec(
                num_scalar_prefetch=1,
                grid=(count * per,),
                in_specs=[tall, flat]
                + [
                    pl.BlockSpec(
                        (chunk, width),
                        lambda step, _, spot=spot, per=per: (
                            jnp.clip(step - spot * per, 0, per - 1),
                            0,
                        ),
                    )
                    for spot in range(count)
                ]
                + [whole(), whole()]
                + [anywhere] * len(updated),
                out_specs=(tall, flat),
            ),
            input_output_aliases={5 + count: 0, 6 + count: 1} if updated else {},
            cost_estimate=cost(2**32, 5 * table_rows * width),
        )(places, item_table, adagrad_state[None, :], *pieces, neg_sum, neg_spots, *updated)
    new_table, new_state = updated

    part = examples // 2
    homes = ()
    for side in range(2):
        tall = pl.BlockSpec((part, width), lambda step, side=side: (side + step, 0))
        flat = pl.BlockSpec((1, part), lambda step, side=side: (0, side + step))
        homes = pl.pallas_call(
            lambda *refs: home_kernel(table_rows, *refs),
            out_shape=(
                jax.ShapeDtypeStruct((examples, width), BF16),
                jax.ShapeDtypeStruct((1, examples), F32),
            ),
            grid=(1,),
            in_specs=[tall, flat, flat, whole(), whole(), whole()] + [anywhere] * len(homes),
            out_specs=(tall, flat),
            input_output_aliases={6: 0, 7: 1} if homes else {},
            cost_estimate=cost(2**32, 8 * negs * width),
        )(queries, place, own_gid[None, :], back, all_negs, local_ids, *homes)
    query_grad, example_loss = homes
    return (query_grad, example_loss.reshape(examples), new_table, new_state.reshape(table_rows))


def solution(mesh):
    placed = (
        P(("dp", "item"), None),
        P("item", None),
        P("item"),
        P(("dp", "item"), None),
        P(("dp", "item")),
        P(("dp", "item")),
    )

    return jax.shard_map(
        on_device,
        mesh=mesh,
        in_specs=placed,
        out_specs=(P(("dp", "item"), None), P(("dp", "item")), P("item", None), P("item")),
        check_vma=False,
    )
```
